32 devices in a mesh: pipe: 8 (over z, y), head: 4 (over x, core).
Axes of the slice: x: 2, y: 2, z: 4, core: 2. Of those that a mesh axis runs over, the one named last changes fastest.
Arguments:
- queries: bfloat16 [2, 2048, 8192], P(None, 'pipe', 'head'), may hold values from -150 to 150
- keys: bfloat16 [2048, 1024], P(('pipe', 'head')), may hold values from -7 to 7
- values: bfloat16 [2048, 1024], P(('pipe', 'head')), may hold values from -6 to 6
- slice_index: int32 [2, 8], replicated, may hold values from 0 to 7, each once within a row
Outputs:
- attended: bfloat16 [2, 2048, 8192], P(None, 'pipe', 'head')
The draws below stay inside these ranges and needn't reach their ends.
Inputs may be any that keep to these rules, and one draw needn't show every extreme that they name: Each row of slice_index is a permutation of 0 to 7.
All inputs are finite; a program needn't handle non-finite values.
Results may differ from the reference program's by a relative error of at most 0.0041.
Values may be sent and summed in bfloat16 or wider, within the bound.
A program may use at most 128 MiB of HBM per device.

```python
import jax
import jax.numpy as jnp
from jax import lax

QUERY_HEADS = 64
KEY_VALUE_HEADS = 8
HEAD_SIZE = 128
SLICE_ROWS = 256
TICK_COUNT = 2
SEQUENCE_TOKENS = 2048
N_PIPE = 8


def key_region(key):
    query_field = jax.random.truncated_normal(jax.random.fold_in(key, 11), -6.0, 6.0, (SEQUENCE_TOKENS, KEY_VALUE_HEADS * HEAD_SIZE), jnp.float32)
    return query_field


def draw_keys(key, part):
    return key_region(key).astype(jnp.bfloat16)


def draw_queries(key, part):
    query_field = jax.random.truncated_normal(jax.random.fold_in(key, 21), -6.0, 6.0, (TICK_COUNT, SEQUENCE_TOKENS, QUERY_HEADS * HEAD_SIZE), jnp.float32)
    return query_field.astype(jnp.bfloat16)


def levels(rng, shape, split, least, largest):
    loudness, own = 1.0, jax.random.fold_in(rng, 6)
    for axis_at, shards_of in split:
        draws = jnp.exp(jax.random.uniform(jax.random.fold_in(own, axis_at), (shards_of,), jnp.float32, least / len(split), largest / len(split)))
        loudness = loudness * jnp.repeat(draws, shape[axis_at] // shards_of).reshape([-1 if axis == axis_at else 1 for axis in range(len(shape))])
    return loudness


def centred(own_key, shape, width, reach, shards=(), kind=jnp.bfloat16):
    result = width * jax.random.normal(own_key, shape, jnp.float32)
    if shards:
        result = result * levels(own_key, shape, shards, -0.22, 0.18)
    return jnp.clip(result, -reach, reach).astype(kind)


def setup_inputs(seed: int = 0) -> dict:
    seeds = jax.random.split(jax.random.key(seed), 5)
    return {
        "queries": draw_queries(jax.random.fold_in(seeds[4], 71), 0),
        "keys": draw_keys(jax.random.fold_in(seeds[4], 71), 0),
        "values": centred(seeds[2], (SEQUENCE_TOKENS, KEY_VALUE_HEADS * HEAD_SIZE), 1.0, 6.0, ((0, 32),)),
        "slice_index": jax.vmap(lambda own: jax.random.permutation(own, N_PIPE))(jax.random.split(seeds[3], TICK_COUNT)).reshape((TICK_COUNT, N_PIPE)).astype(jnp.int32),
    }


NEG = -1.0e30


def reference(queries, keys, values, slice_index):
    query_group = QUERY_HEADS // KEY_VALUE_HEADS
    query_matrix = queries.reshape(TICK_COUNT, N_PIPE, SLICE_ROWS, KEY_VALUE_HEADS, query_group, HEAD_SIZE)
    key_matrix = keys.reshape(SEQUENCE_TOKENS, KEY_VALUE_HEADS, HEAD_SIZE)
    value_matrix = values.reshape(SEQUENCE_TOKENS, KEY_VALUE_HEADS, HEAD_SIZE)
    key_pos = jnp.arange(SEQUENCE_TOKENS, dtype=jnp.int32)

    def single_output(item_index):
        tick_index = item_index // (N_PIPE * KEY_VALUE_HEADS)
        section_index = (item_index // KEY_VALUE_HEADS) % N_PIPE
        head_index = item_index % KEY_VALUE_HEADS
        query = query_matrix[tick_index, section_index, :, head_index].astype(jnp.float32)
        key_head = key_matrix[:, head_index].astype(jnp.float32)
        value_head = value_matrix[:, head_index].astype(jnp.float32)
        query_pos = slice_index[tick_index, section_index].astype(jnp.int32) * SLICE_ROWS + jnp.arange(SLICE_ROWS, dtype=jnp.int32)
        scores = jnp.einsum("rgd,kd->rgk", query, key_head) * (HEAD_SIZE ** -0.5)
        allowed = (key_pos[None, :] <= query_pos[:, None])[:, None, :]
        peak = jnp.max(jnp.where(allowed, scores, NEG), axis=-1)
        weights = jnp.where(allowed, jnp.exp(scores - peak[..., None]), 0.0)
        total = jnp.sum(weights, axis=-1)
        numer = jnp.einsum("rgk,kd->rgd", weights.astype(jnp.bfloat16).astype(jnp.float32), value_head)
        return (numer / total[..., None]).astype(jnp.bfloat16)

    output_list = lax.map(single_output, jnp.arange(TICK_COUNT * N_PIPE * KEY_VALUE_HEADS, dtype=jnp.int32))
    output_list = output_list.reshape(TICK_COUNT, N_PIPE, KEY_VALUE_HEADS, SLICE_ROWS, query_group, HEAD_SIZE).transpose(0, 1, 3, 2, 4, 5)
    return output_list.reshape(TICK_COUNT, SEQUENCE_TOKENS, QUERY_HEADS * HEAD_SIZE)
```

```python
import math

import jax
import jax.numpy as jnp
from jax import lax
from jax.experimental import pallas as pl
from jax.experimental.pallas import tpu as pltpu
from jax.sharding import PartitionSpec as P

HEAD_SIZE = 128
NEG = -1e30
TO_EXP2 = HEAD_SIZE ** (-0.5) * math.log2(math.e)
MESH = pl.DeviceIdType.MESH
STRIP = 4


def scores_of(query, key_block):
    return lax.dot_general(query, key_block, (((1,), (1,)), ((), ())), preferred_element_type=jnp.float32)


def weigh(scores, peak, value_block):
    weights = jnp.exp2((scores - peak) * TO_EXP2).astype(jnp.bfloat16)
    ones = jnp.ones(value_block.shape, jnp.bfloat16)
    return jnp.dot(weights, jnp.concatenate([value_block, ones], axis=1), preferred_element_type=jnp.float32)


def wide(array, count):
    return jnp.concatenate([array] * count, axis=1)


def fused_kernel(n_pipe, n_head, index_ref, q_ref, k_ref, v_ref, o_ref, kbuf, vbuf, qbuf, obuf, best_ref, accum_ref,
                 local_sem, head_send, head_recv, left_send, right_send, side_send, chunk_recv, q_sem, out_sem):
    me = lax.axis_index("pipe")
    head = lax.axis_index("head")
    side = me + 1 - 2 * lax.rem(me, 2)
    row = lax.div(me, 2)
    line = n_pipe // 2
    has_left, has_right = row > 0, row < line - 1
    piece = k_ref.shape[0]
    rows = piece * n_head
    near_heads = n_head // 2
    half_rows = rows // 2
    mine = lax.div(head, near_heads)
    width = kbuf.shape[1]
    ins, bufs = (k_ref, v_ref), (kbuf, vbuf)

    barrier = pltpu.get_barrier_semaphore()
    for other in range(1, n_head):
        pl.semaphore_signal(barrier, inc=1, device_id=(me, lax.rem(head + other, n_head)), device_id_type=MESH)
    pl.semaphore_signal(barrier, inc=1, device_id=(side, head), device_id_type=MESH)

    @pl.when(has_left)
    def _():
        pl.semaphore_signal(barrier, inc=1, device_id=(me - 2, head), device_id_type=MESH)

    @pl.when(has_right)
    def _():
        pl.semaphore_signal(barrier, inc=1, device_id=(me + 2, head), device_id_type=MESH)

    def spot(kind, source):
        return bufs[kind].at[pl.ds(pl.multiple_of(me * rows + source * piece, piece), piece), :]

    def columns(kind, target):
        return ins[kind].at[:, pl.ds(pl.multiple_of(target * width, width), width)]

    def keep(kind):
        return pltpu.make_async_copy(columns(kind, head), spot(kind, head), local_sem.at[kind])

    for kind in range(2):
        keep(kind).start()
    pltpu.make_async_copy(q_ref, qbuf, q_sem).start()
    pl.semaphore_wait(barrier, n_head + jnp.where(has_left, 1, 0) + jnp.where(has_right, 1, 0))

    def chunk(kind, owner, half):
        return bufs[kind].at[pl.ds(pl.multiple_of(owner * rows + half * half_rows, half_rows), half_rows), :]

    def partner(far, shift):
        group = lax.rem(mine + far, 2)
        return group * near_heads + lax.rem(lax.rem(head, near_heads) + shift, near_heads)

    def exchange(kind, far, shift):
        target = partner(far, shift)
        return pltpu.make_async_remote_copy(
            columns(kind, target), spot(kind, head),
            head_send.at[kind, far, shift], head_recv.at[kind, far, shift],
            device_id=(me, target), device_id_type=MESH)

    def arrival(kind, far, shift):
        source = partner(far, near_heads - shift)
        return pltpu.make_async_remote_copy(
            columns(kind, head), spot(kind, source),
            head_send.at[kind, far, shift], head_recv.at[kind, far, shift],
            device_id=(me, source), device_id_type=MESH)

    def pass_on(kind, owner, half, target, sems):
        return pltpu.make_async_remote_copy(
            chunk(kind, owner, half), chunk(kind, owner, half), sems.at[kind, owner, half], chunk_recv.at[kind, owner, half],
            device_id=(target, head), device_id_type=MESH)

    def to_left(kind, owner, half):
        return pass_on(kind, owner, half, me - 2, left_send)

    def to_right(kind, owner, half):
        return pass_on(kind, owner, half, me + 2, right_send)

    def to_side(kind, owner, half):
        return pass_on(kind, owner, half, side, side_send)

    for kind in range(2):
        for shift in range(1, near_heads):
            exchange(kind, 0, shift).start()
    for kind in range(2):
        for shift in range(near_heads):
            exchange(kind, 1, shift).start()

    def spread(kind, half):
        to_side(kind, me, half).start()

        @pl.when(has_left)
        def _():
            to_left(kind, me, half).start()

        @pl.when(has_right)
        def _():
            to_right(kind, me, half).start()

    for kind in range(2):
        keep(kind).wait()
        for shift in range(1, near_heads):
            arrival(kind, 0, shift).wait_recv()
        spread(kind, mine)
    for kind in range(2):
        for shift in range(near_heads):
            arrival(kind, 1, shift).wait_recv()
        spread(kind, 1 - mine)

    def halves(order):
        return mine if order == 0 else 1 - mine

    def relay(distance, order):
        half = halves(order)
        has_before, has_after = row >= distance, row + distance < line
        before, after = me - 2 * distance, me + 2 * distance

        @pl.when(has_before)
        def _():
            for kind in range(2):
                to_right(kind, before, half).wait_recv()

                @pl.when(has_right)
                def _():
                    to_right(kind, before, half).start()

                to_side(kind, before, half).start()

        @pl.when(has_after)
        def _():
            for kind in range(2):
                to_left(kind, after, half).wait_recv()

                @pl.when(has_left)
                def _():
                    to_left(kind, after, half).start()

        if order == 0:

            @pl.when(jnp.logical_and(has_after, jnp.logical_not(has_before)))
            def _():
                for kind in range(2):
                    to_side(kind, after, half).start()
        else:

            @pl.when(has_after)
            def _():
                @pl.when(has_before)
                def _():
                    for kind in range(2):
                        to_side(kind, after, mine).start()

                for kind in range(2):
                    to_side(kind, after, half).start()

    ticks, _, q_width = qbuf.shape
    heads = q_width // HEAD_SIZE
    kv_heads = width // HEAD_SIZE
    group = heads // kv_heads
    diff = lax.broadcasted_iota(jnp.int32, (rows, rows), 1) - lax.broadcasted_iota(jnp.int32, (rows, rows), 0)
    reach = jnp.minimum(row, line - 1 - row)

    def nearest(place):
        offset = lax.div(place + 1, 2)
        near = jnp.where(lax.rem(place, 2) == 1, row - offset, row + offset)
        far = jnp.where(row < line - 1 - row, place, line - 1 - place)
        return jnp.where(place <= 2 * reach, near, far)

    strips = heads // STRIP

    def strip_out(tick, strip):
        at = pl.ds(strip * STRIP * HEAD_SIZE, STRIP * HEAD_SIZE)
        return pltpu.make_async_copy(obuf.at[tick, :, at], o_ref.at[tick, :, at], out_sem.at[tick, strip])

    def compute(chunks, first, last, before_tick):
        spans = [pl.ds(pl.multiple_of(owner * rows, rows), rows) for owner in chunks]

        @pl.loop(0, ticks)
        def _(tick):
            before_tick(tick)
            start = index_ref[tick, me] * rows
            for h in range(heads):
                at = pl.ds(h * HEAD_SIZE, HEAD_SIZE)
                kv = pl.ds(h // group * HEAD_SIZE, HEAD_SIZE)
                slot = tick * heads + h
                query = qbuf[tick, :, at]
                scores = wide_join([
                    jnp.where(diff <= start - owner * rows, scores_of(query, kbuf[span, kv]), NEG)
                    for owner, span in zip(chunks, spans)
                ], 1)
                top = jnp.broadcast_to(jnp.max(scores, axis=-1, keepdims=True), (rows, HEAD_SIZE))
                if first:
                    peak = top
                else:
                    before = best_ref[slot]
                    peak = jnp.maximum(before, top)
                block = wide_join([vbuf[span, kv] for span in spans], 0)
                result = weigh(scores, wide(peak, len(chunks) * rows // HEAD_SIZE), block)
                if not first:
                    result = result + accum_ref[slot] * wide(jnp.exp2((before - peak) * TO_EXP2), 2)
                if last:
                    obuf[tick, :, at] = (result[:, :HEAD_SIZE] / result[:, HEAD_SIZE:]).astype(obuf.dtype)
                    if h % STRIP == STRIP - 1:
                        strip_out(tick, h // STRIP).start()
                else:
                    best_ref[slot] = peak
                    accum_ref[slot] = result

    def side_owner(place):
        return 2 * nearest(place) + lax.rem(side, 2)

    def own_owner(place):
        return 2 * nearest(place) + lax.rem(me, 2)

    def side_wait(owner):
        for half in range(2):
            for kind in range(2):
                to_side(kind, owner, half).wait_recv()

    def first_events(tick):
        @pl.when(tick == 0)
        def _():
            relay(1, 0)

    relay_at = first_events
    pltpu.make_async_copy(q_ref, qbuf, q_sem).wait()
    compute([me], True, False, relay_at)

    @pl.loop(1, line)
    def _(step):
        def events(tick):
            @pl.when(tick == 0)
            def _():
                relay(step, 1)
                side_wait(side_owner(step - 1))

            @pl.when(tick == 1)
            def _():
                relay(step + 1, 0)

        compute([own_owner(step), side_owner(step - 1)], False, False, events)

    def last_events(tick):
        @pl.when(tick == 0)
        def _():
            side_wait(side_owner(line - 1))

    compute([side_owner(line - 1)], False, True, last_events)

    for kind in range(2):
        for shift in range(1, near_heads):
            exchange(kind, 0, shift).wait_send()
        for shift in range(near_heads):
            exchange(kind, 1, shift).wait_send()

    @pl.loop(0, line)
    def _(index):
        owner = 2 * index + lax.rem(me, 2)
        for half in range(2):
            for kind in range(2):
                to_side(kind, owner, half).wait_send()

                @pl.when(jnp.logical_and(has_right, index <= row))
                def _():
                    to_right(kind, owner, half).wait_send()

                @pl.when(jnp.logical_and(has_left, index >= row))
                def _():
                    to_left(kind, owner, half).wait_send()

    for tick in range(ticks):
        for strip in range(strips):
            strip_out(tick, strip).wait()


def wide_join(parts, axis):
    return parts[0] if len(parts) == 1 else jnp.concatenate(parts, axis=axis)


def on_device(sizes, queries, keys, values, slice_index):
    n_pipe, n_head = sizes
    ticks, rows, columns = queries.shape
    shape = (rows * n_pipe, keys.shape[1] // n_head)
    slots = ticks * columns // HEAD_SIZE
    anywhere = pl.BlockSpec(memory_space=pl.ANY)
    dma = pltpu.SemaphoreType.DMA
    return pl.pallas_call(
        lambda *refs: fused_kernel(n_pipe, n_head, *refs),
        out_shape=jax.ShapeDtypeStruct(queries.shape, queries.dtype),
        in_specs=[pl.BlockSpec(memory_space=pltpu.SMEM), anywhere, anywhere, anywhere],
        out_specs=anywhere,
        scratch_shapes=[
            pltpu.VMEM(shape, keys.dtype),
            pltpu.VMEM(shape, keys.dtype),
            pltpu.VMEM(queries.shape, queries.dtype),
            pltpu.VMEM(queries.shape, queries.dtype),
            pltpu.VMEM((slots, rows, HEAD_SIZE), jnp.float32),
            pltpu.VMEM((slots, rows, 2 * HEAD_SIZE), jnp.float32),
            dma((2,)),
            dma((2, 2, n_head // 2)),
            dma((2, 2, n_head // 2)),
            dma((2, n_pipe, 2)),
            dma((2, n_pipe, 2)),
            dma((2, n_pipe, 2)),
            dma((2, n_pipe, 2)),
            dma,
            dma((ticks, columns // HEAD_SIZE // STRIP)),
        ],
        compiler_params=pltpu.CompilerParams(collective_id=0, has_side_effects=True, vmem_limit_bytes=60 * 2 ** 20),
        name="fused",
    )(slice_index, queries, keys, values)


def solution(mesh):
    sizes = (mesh.shape["pipe"], mesh.shape["head"])
    return jax.shard_map(
        lambda *arrays: on_device(sizes, *arrays),
        mesh=mesh,
        in_specs=(
            P(None, "pipe", "head"),
            P(("pipe", "head"), None),
            P(("pipe", "head"), None),
            P(),
        ),
        out_specs=P(None, "pipe", "head"),
        check_vma=False,
    )
```

```python
import math

import jax
import jax.numpy as jnp
from jax import lax
from jax.experimental import pallas as pl
from jax.experimental.pallas import tpu as pltpu
from jax.sharding import PartitionSpec as P

HEAD_SIZE = 128
NEG = -1e30
TO_EXP2 = HEAD_SIZE ** (-0.5) * math.log2(math.e)
MESH = pl.DeviceIdType.MESH
STRIP = 4


def scores_of(query, key_block):
    return lax.dot_general(query, key_block, (((1,), (1,)), ((), ())), preferred_element_type=jnp.float32)


def weigh(scores, peak, value_block):
    weights = jnp.exp2((scores - peak) * TO_EXP2).astype(jnp.bfloat16)
    ones = jnp.ones(value_block.shape, jnp.bfloat16)
    return jnp.dot(weights, jnp.concatenate([value_block, ones], axis=1), preferred_element_type=jnp.float32)


def wide(array, count):
    return jnp.concatenate([array] * count, axis=1)


def fused_kernel(n_pipe, n_head, slice_ref, q_ref, k_ref, v_ref, o_ref, kbuf, vbuf, qbuf, obuf, best_ref, accum_ref,
                 index_ref, index_sem, local_sem, head_send, head_recv, left_send, right_send, side_send, chunk_recv, q_sem, out_sem):
    me = lax.axis_index("pipe")
    head = lax.axis_index("head")
    side = me + 1 - 2 * lax.rem(me, 2)
    row = lax.div(me, 2)
    line = n_pipe // 2
    has_left, has_right = row > 0, row < line - 1
    piece = k_ref.shape[0]
    rows = piece * n_head
    near_heads = n_head // 2
    half_rows = rows // 2
    mine = lax.div(head, near_heads)
    width = kbuf.shape[1]
    ins, bufs = (k_ref, v_ref), (kbuf, vbuf)

    barrier = pltpu.get_barrier_semaphore()
    for other in range(1, n_head):
        pl.semaphore_signal(barrier, inc=1, device_id=(me, lax.rem(head + other, n_head)), device_id_type=MESH)
    pl.semaphore_signal(barrier, inc=1, device_id=(side, head), device_id_type=MESH)

    @pl.when(has_left)
    def _():
        pl.semaphore_signal(barrier, inc=1, device_id=(me - 2, head), device_id_type=MESH)

    @pl.when(has_right)
    def _():
        pl.semaphore_signal(barrier, inc=1, device_id=(me + 2, head), device_id_type=MESH)

    def spot(kind, source):
        return bufs[kind].at[pl.ds(pl.multiple_of(me * rows + source * piece, piece), piece), :]

    def columns(kind, target):
        return ins[kind].at[:, pl.ds(pl.multiple_of(target * width, width), width)]

    def keep(kind):
        return pltpu.make_async_copy(columns(kind, head), spot(kind, head), local_sem.at[kind])

    for kind in range(2):
        keep(kind).start()
    pltpu.make_async_copy(slice_ref, index_ref, index_sem).start()
    pltpu.make_async_copy(q_ref, qbuf, q_sem).start()
    pl.semaphore_wait(barrier, n_head + jnp.where(has_left, 1, 0) + jnp.where(has_right, 1, 0))

    def chunk(kind, owner, half):
        return bufs[kind].at[pl.ds(pl.multiple_of(owner * rows + half * half_rows, half_rows), half_rows), :]

    def partner(far, shift):
        group = lax.rem(mine + far, 2)
        return group * near_heads + lax.rem(lax.rem(head, near_heads) + shift, near_heads)

    def exchange(kind, far, shift):
        target = partner(far, shift)
        return pltpu.make_async_remote_copy(
            columns(kind, target), spot(kind, head),
            head_send.at[kind, far, shift], head_recv.at[kind, far, shift],
            device_id=(me, target), device_id_type=MESH)

    def arrival(kind, far, shift):
        source = partner(far, near_heads - shift)
        return pltpu.make_async_remote_copy(
            columns(kind, head), spot(kind, source),
            head_send.at[kind, far, shift], head_recv.at[kind, far, shift],
            device_id=(me, source), device_id_type=MESH)

    def pass_on(kind, owner, half, target, sems):
        return pltpu.make_async_remote_copy(
            chunk(kind, owner, half), chunk(kind, owner, half), sems.at[kind, owner, half], chunk_recv.at[kind, owner, half],
            device_id=(target, head), device_id_type=MESH)

    def to_left(kind, owner, half):
        return pass_on(kind, owner, half, me - 2, left_send)

    def to_right(kind, owner, half):
        return pass_on(kind, owner, half, me + 2, right_send)

    def to_side(kind, owner, half):
        return pass_on(kind, owner, half, side, side_send)

    for kind in range(2):
        for shift in range(1, near_heads):
            exchange(kind, 0, shift).start()
    for kind in range(2):
        for shift in range(near_heads):
            exchange(kind, 1, shift).start()

    def spread(kind, half):
        to_side(kind, me, half).start()

        @pl.when(has_left)
        def _():
            to_left(kind, me, half).start()

        @pl.when(has_right)
        def _():
            to_right(kind, me, half).start()

    for kind in range(2):
        keep(kind).wait()
        for shift in range(1, near_heads):
            arrival(kind, 0, shift).wait_recv()
        spread(kind, mine)
    for kind in range(2):
        for shift in range(near_heads):
            arrival(kind, 1, shift).wait_recv()
        spread(kind, 1 - mine)

    def halves(order):
        return mine if order == 0 else 1 - mine

    def is_end(at):
        return jnp.logical_or(at == 0, at == line - 1)

    def crosses(at, order):
        return True if order == 0 else jnp.logical_or(jnp.logical_not(is_end(at)), at == row)

    def relay(distance, order):
        half = halves(order)
        has_before, has_after = row >= distance, row + distance < line
        before, after = me - 2 * distance, me + 2 * distance

        @pl.when(has_before)
        def _():
            for kind in range(2):
                to_right(kind, before, half).wait_recv()

                @pl.when(has_right)
                def _():
                    to_right(kind, before, half).start()

                @pl.when(crosses(row - distance, order))
                def _():
                    to_side(kind, before, half).start()

        @pl.when(has_after)
        def _():
            for kind in range(2):
                to_left(kind, after, half).wait_recv()

                @pl.when(has_left)
                def _():
                    to_left(kind, after, half).start()

        if order == 0:

            @pl.when(jnp.logical_and(has_after, jnp.logical_not(has_before)))
            def _():
                for kind in range(2):
                    to_side(kind, after, half).start()
        else:

            @pl.when(jnp.logical_and(has_after, has_before))
            def _():
                for kind in range(2):
                    to_side(kind, after, mine).start()

            @pl.when(jnp.logical_and(has_after, crosses(row + distance, order)))
            def _():
                for kind in range(2):
                    to_side(kind, after, half).start()

    first_side, last_side = lax.rem(side, 2), 2 * (line - 1) + lax.rem(side, 2)

    def guests_start():
        for kind in range(2):

            @pl.when(row == 0)
            def _():
                to_right(kind, first_side, 1 - mine).start()

            @pl.when(row == line - 1)
            def _():
                to_left(kind, last_side, 1 - mine).start()

    def guests_pass(distance):
        for kind in range(2):

            @pl.when(row == distance)
            def _():
                to_right(kind, first_side, 1 - mine).wait_recv()

                @pl.when(has_right)
                def _():
                    to_right(kind, first_side, 1 - mine).start()

            @pl.when(row == line - 1 - distance)
            def _():
                to_left(kind, last_side, 1 - mine).wait_recv()

                @pl.when(has_left)
                def _():
                    to_left(kind, last_side, 1 - mine).start()

    ticks, _, q_width = qbuf.shape
    heads = q_width // HEAD_SIZE
    kv_heads = width // HEAD_SIZE
    group = heads // kv_heads
    diff = lax.broadcasted_iota(jnp.int32, (rows, rows), 1) - lax.broadcasted_iota(jnp.int32, (rows, rows), 0)
    reach = jnp.minimum(row, line - 1 - row)

    def nearest(place):
        offset = lax.div(place + 1, 2)
        near = jnp.where(lax.rem(place, 2) == 1, row - offset, row + offset)
        far = jnp.where(row < line - 1 - row, place, line - 1 - place)
        return jnp.where(place <= 2 * reach, near, far)

    strips = heads // STRIP

    def strip_out(tick, strip):
        at = pl.ds(strip * STRIP * HEAD_SIZE, STRIP * HEAD_SIZE)
        return pltpu.make_async_copy(obuf.at[tick, :, at], o_ref.at[tick, :, at], out_sem.at[tick, strip])

    def compute(chunks, first, last, before_tick):
        spans = [pl.ds(pl.multiple_of(owner * rows, rows), rows) for owner in chunks]

        @pl.loop(0, ticks)
        def _(tick):
            before_tick(tick)
            start = index_ref[tick, me] * rows
            for h in range(heads):
                at = pl.ds(h * HEAD_SIZE, HEAD_SIZE)
                kv = pl.ds(h // group * HEAD_SIZE, HEAD_SIZE)
                slot = tick * heads + h
                query = qbuf[tick, :, at]
                scores = wide_join([
                    jnp.where(diff <= start - owner * rows, scores_of(query, kbuf[span, kv]), NEG)
                    for owner, span in zip(chunks, spans)
                ], 1)
                top = jnp.broadcast_to(jnp.max(scores, axis=-1, keepdims=True), (rows, HEAD_SIZE))
                if first:
                    peak = top
                else:
                    before = best_ref[slot]
                    peak = jnp.maximum(before, top)
                block = wide_join([vbuf[span, kv] for span in spans], 0)
                result = weigh(scores, wide(peak, len(chunks) * rows // HEAD_SIZE), block)
                if not first:
                    result = result + accum_ref[slot] * wide(jnp.exp2((before - peak) * TO_EXP2), 2)
                if last:
                    obuf[tick, :, at] = (result[:, :HEAD_SIZE] / result[:, HEAD_SIZE:]).astype(obuf.dtype)
                    if h % STRIP == STRIP - 1:
                        strip_out(tick, h // STRIP).start()
                else:
                    best_ref[slot] = peak
                    accum_ref[slot] = result

    def side_owner(place):
        return 2 * nearest(place) + lax.rem(side, 2)

    def own_owner(place):
        return 2 * nearest(place) + lax.rem(me, 2)

    def side_wait(owner):
        for order in range(2):

            @pl.when(crosses(lax.div(owner, 2), order))
            def _():
                for kind in range(2):
                    to_side(kind, owner, halves(order)).wait_recv()

    def first_events(tick):
        @pl.when(tick == 0)
        def _():
            relay(1, 0)

    relay_at = first_events
    pltpu.make_async_copy(slice_ref, index_ref, index_sem).wait()
    pltpu.make_async_copy(q_ref, qbuf, q_sem).wait()
    compute([me], True, False, relay_at)

    @pl.loop(1, line)
    def _(step):
        def events(tick):
            @pl.when(tick == 0)
            def _():
                relay(step, 1)
                side_wait(side_owner(step - 1))

                @pl.when(step == 1)
                def _():
                    guests_start()

                @pl.when(step > 1)
                def _():
                    guests_pass(step - 1)

            @pl.when(tick == 1)
            def _():
                relay(step + 1, 0)

        compute([own_owner(step), side_owner(step - 1)], False, False, events)

    def last_events(tick):
        @pl.when(tick == 0)
        def _():
            side_wait(side_owner(line - 1))
            guests_pass(line - 1)

    compute([side_owner(line - 1)], False, True, last_events)

    for kind in range(2):
        for shift in range(1, near_heads):
            exchange(kind, 0, shift).wait_send()
        for shift in range(near_heads):
            exchange(kind, 1, shift).wait_send()

    @pl.loop(0, line)
    def _(index):
        owner = 2 * index + lax.rem(me, 2)
        for order in range(2):
            half = halves(order)
            for kind in range(2):

                @pl.when(crosses(index, order))
                def _():
                    to_side(kind, owner, half).wait_send()

                @pl.when(jnp.logical_and(has_right, index <= row))
                def _():
                    to_right(kind, owner, half).wait_send()

                @pl.when(jnp.logical_and(has_left, index >= row))
                def _():
                    to_left(kind, owner, half).wait_send()

    for kind in range(2):

        @pl.when(has_right)
        def _():
            to_right(kind, first_side, 1 - mine).wait_send()

        @pl.when(has_left)
        def _():
            to_left(kind, last_side, 1 - mine).wait_send()

    for tick in range(ticks):
        for strip in range(strips):
            strip_out(tick, strip).wait()


def wide_join(parts, axis):
    return parts[0] if len(parts) == 1 else jnp.concatenate(parts, axis=axis)


def on_device(sizes, queries, keys, values, slice_index):
    n_pipe, n_head = sizes
    ticks, rows, columns = queries.shape
    shape = (rows * n_pipe, keys.shape[1] // n_head)
    slots = ticks * columns // HEAD_SIZE
    anywhere = pl.BlockSpec(memory_space=pl.ANY)
    dma = pltpu.SemaphoreType.DMA
    return pl.pallas_call(
        lambda *refs: fused_kernel(n_pipe, n_head, *refs),
        out_shape=jax.ShapeDtypeStruct(queries.shape, queries.dtype),
        in_specs=[anywhere] * 4,
        out_specs=anywhere,
        scratch_shapes=[
            pltpu.VMEM(shape, keys.dtype),
            pltpu.VMEM(shape, keys.dtype),
            pltpu.VMEM(queries.shape, queries.dtype),
            pltpu.VMEM(queries.shape, queries.dtype),
            pltpu.VMEM((slots, rows, HEAD_SIZE), jnp.float32),
            pltpu.VMEM((slots, rows, 2 * HEAD_SIZE), jnp.float32),
            pltpu.SMEM(slice_index.shape, slice_index.dtype),
            dma,
            dma((2,)),
            dma((2, 2, n_head // 2)),
            dma((2, 2, n_head // 2)),
            dma((2, n_pipe, 2)),
            dma((2, n_pipe, 2)),
            dma((2, n_pipe, 2)),
            dma((2, n_pipe, 2)),
            dma,
            dma((ticks, columns // HEAD_SIZE // STRIP)),
        ],
        compiler_params=pltpu.CompilerParams(collective_id=0, has_side_effects=True, vmem_limit_bytes=60 * 2 ** 20),
        name="fused",
    )(slice_index, queries, keys, values)


def solution(mesh):
    sizes = (mesh.shape["pipe"], mesh.shape["head"])
    return jax.shard_map(
        lambda *arrays: on_device(sizes, *arrays),
        mesh=mesh,
        in_specs=(
            P(None, "pipe", "head"),
            P(("pipe", "head"), None),
            P(("pipe", "head"), None),
            P(),
        ),
        out_specs=P(None, "pipe", "head"),
        check_vma=False,
    )
```

```python
import math

import jax
import jax.numpy as jnp
from jax import lax
from jax.experimental import pallas as pl
from jax.experimental.pallas import tpu as pltpu
from jax.sharding import PartitionSpec as P

HEAD_SIZE = 128
NEG = -1e30
TO_EXP2 = HEAD_SIZE ** (-0.5) * math.log2(math.e)
MESH = pl.DeviceIdType.MESH
STRIP = 4


def scores_of(query, key_block):
    return lax.dot_general(query, key_block, (((1,), (1,)), ((), ())), preferred_element_type=jnp.float32)


def weigh(scores, peak, value_block):
    weights = jnp.exp2((scores - peak) * TO_EXP2).astype(jnp.bfloat16)
    ones = jnp.ones(value_block.shape, jnp.bfloat16)
    return jnp.dot(weights, jnp.concatenate([value_block, ones], axis=1), preferred_element_type=jnp.float32)


def wide(array, count):
    return jnp.concatenate([array] * count, axis=1)


def nearest(row, line, place):
    reach = jnp.minimum(row, line - 1 - row)
    offset = lax.div(place + 1, 2)
    near = jnp.where(lax.rem(place, 2) == 1, row - offset, row + offset)
    far = jnp.where(row < line - 1 - row, place, line - 1 - place)
    return jnp.where(place <= 2 * reach, near, far)


def attend(tick, start, chunks, rows, first, qbuf, kbuf, vbuf, best_ref, accum_ref, finish):
    spans = [pl.ds(pl.multiple_of(owner * rows, rows), rows) for owner in chunks]
    heads = qbuf.shape[2] // HEAD_SIZE
    group = heads // (kbuf.shape[1] // HEAD_SIZE)
    diff = lax.broadcasted_iota(jnp.int32, (rows, rows), 1) - lax.broadcasted_iota(jnp.int32, (rows, rows), 0)

    limits = wide_join([jnp.where(diff <= start - owner * rows, -NEG, NEG) for owner in chunks], 1)

    def score(h):
        at = pl.ds(h * HEAD_SIZE, HEAD_SIZE)
        kv = pl.ds(h // group * HEAD_SIZE, HEAD_SIZE)
        query = qbuf[tick, :, at]
        scores = wide_join([scores_of(query, kbuf[span, kv]) for span in spans], 1)
        return jnp.minimum(scores, limits)

    def rest(h, scores):
        kv = pl.ds(h // group * HEAD_SIZE, HEAD_SIZE)
        slot = tick * heads + h
        top = jnp.broadcast_to(jnp.max(scores, axis=-1, keepdims=True), (rows, HEAD_SIZE))
        if first:
            peak = top
        else:
            before = best_ref[slot]
            peak = jnp.maximum(before, top)
        block = wide_join([vbuf[span, kv] for span in spans], 0)
        result = weigh(scores, wide(peak, len(chunks) * rows // HEAD_SIZE), block)
        if not first:
            result = result + accum_ref[slot] * wide(jnp.exp2((before - peak) * TO_EXP2), 2)
        if finish is not None:
            finish(h, result)
        else:
            best_ref[slot] = peak
            accum_ref[slot] = result

    scores = score(0)
    for h in range(heads):
        later = score(h + 1) if h + 1 < heads else None
        rest(h, scores)
        scores = later


def finish_kernel(n_pipe, index_ref, kbuf, vbuf, qbuf, best_ref, accum_ref, o_ref, obuf, out_sem):
    me = lax.axis_index("pipe")
    row, line = lax.div(me, 2), n_pipe // 2
    ticks, rows, q_width = qbuf.shape
    heads = q_width // HEAD_SIZE
    owner = 2 * nearest(row, line, line - 1) + 1 - lax.rem(me, 2)

    def strip_out(tick, strip):
        at = pl.ds(strip * STRIP * HEAD_SIZE, STRIP * HEAD_SIZE)
        return pltpu.make_async_copy(obuf.at[tick, :, at], o_ref.at[tick, :, at], out_sem.at[tick, strip])

    @pl.loop(0, ticks)
    def _(tick):
        def finish(h, result):
            obuf[tick, :, pl.ds(h * HEAD_SIZE, HEAD_SIZE)] = (result[:, :HEAD_SIZE] / result[:, HEAD_SIZE:]).astype(obuf.dtype)
            if h % STRIP == STRIP - 1:
                strip_out(tick, h // STRIP).start()

        slice_at = index_ref[tick, me]

        @pl.when(owner <= slice_at)
        def _():
            attend(tick, slice_at * rows, [owner], rows, False, qbuf, kbuf, vbuf, best_ref, accum_ref, finish)

        @pl.when(owner > slice_at)
        def _():
            for h in range(heads):
                finish(h, accum_ref[tick * heads + h])

    for tick in range(ticks):
        for strip in range(heads // STRIP):
            strip_out(tick, strip).wait()


def gather_kernel(n_pipe, n_head, slice_ref, q_ref, k_ref, v_ref, kbuf, vbuf, qbuf, best_ref, accum_ref,
                  index_ref, index_sem, local_sem, head_send, head_recv, left_send, right_send, side_send, chunk_recv, q_sem):
    me = lax.axis_index("pipe")
    head = lax.axis_index("head")
    side = me + 1 - 2 * lax.rem(me, 2)
    row = lax.div(me, 2)
    line = n_pipe // 2
    has_left, has_right = row > 0, row < line - 1
    piece = k_ref.shape[0]
    rows = piece * n_head
    near_heads = n_head // 2
    half_rows = rows // 2
    mine = lax.div(head, near_heads)
    width = kbuf.shape[1]
    ins, bufs = (k_ref, v_ref), (kbuf, vbuf)

    barrier = pltpu.get_barrier_semaphore()
    for other in range(1, n_head):
        pl.semaphore_signal(barrier, inc=1, device_id=(me, lax.rem(head + other, n_head)), device_id_type=MESH)
    pl.semaphore_signal(barrier, inc=1, device_id=(side, head), device_id_type=MESH)

    @pl.when(has_left)
    def _():
        pl.semaphore_signal(barrier, inc=1, device_id=(me - 2, head), device_id_type=MESH)

    @pl.when(has_right)
    def _():
        pl.semaphore_signal(barrier, inc=1, device_id=(me + 2, head), device_id_type=MESH)

    def spot(kind, source):
        return bufs[kind].at[pl.ds(pl.multiple_of(me * rows + source * piece, piece), piece), :]

    def columns(kind, target):
        return ins[kind].at[:, pl.ds(pl.multiple_of(target * width, width), width)]

    def keep(kind):
        return pltpu.make_async_copy(columns(kind, head), spot(kind, head), local_sem.at[kind])

    for kind in range(2):
        keep(kind).start()
    pltpu.make_async_copy(slice_ref, index_ref, index_sem).start()
    pltpu.make_async_copy(q_ref, qbuf, q_sem).start()
    pl.semaphore_wait(barrier, n_head + jnp.where(has_left, 1, 0) + jnp.where(has_right, 1, 0))

    def chunk(kind, owner, half):
        return bufs[kind].at[pl.ds(pl.multiple_of(owner * rows + half * half_rows, half_rows), half_rows), :]

    def partner(far, shift):
        group = lax.rem(mine + far, 2)
        return group * near_heads + lax.rem(lax.rem(head, near_heads) + shift, near_heads)

    def exchange(kind, far, shift):
        target = partner(far, shift)
        return pltpu.make_async_remote_copy(
            columns(kind, target), spot(kind, head),
            head_send.at[kind, far, shift], head_recv.at[kind, far, shift],
            device_id=(me, target), device_id_type=MESH)

    def arrival(kind, far, shift):
        source = partner(far, near_heads - shift)
        return pltpu.make_async_remote_copy(
            columns(kind, head), spot(kind, source),
            head_send.at[kind, far, shift], head_recv.at[kind, far, shift],
            device_id=(me, source), device_id_type=MESH)

    def pass_on(kind, owner, half, target, sems):
        return pltpu.make_async_remote_copy(
            chunk(kind, owner, half), chunk(kind, owner, half), sems.at[kind, owner, half], chunk_recv.at[kind, owner, half],
            device_id=(target, head), device_id_type=MESH)

    def to_left(kind, owner, half):
        return pass_on(kind, owner, half, me - 2, left_send)

    def to_right(kind, owner, half):
        return pass_on(kind, owner, half, me + 2, right_send)

    def to_side(kind, owner, half):
        return pass_on(kind, owner, half, side, side_send)

    for kind in range(2):
        for shift in range(1, near_heads):
            exchange(kind, 0, shift).start()
    for kind in range(2):
        for shift in range(near_heads):
            exchange(kind, 1, shift).start()

    def spread(kind, half):
        to_side(kind, me, half).start()

        @pl.when(has_left)
        def _():
            to_left(kind, me, half).start()

        @pl.when(has_right)
        def _():
            to_right(kind, me, half).start()

    for kind in range(2):
        keep(kind).wait()
        for shift in range(1, near_heads):
            arrival(kind, 0, shift).wait_recv()
        spread(kind, mine)
    for kind in range(2):
        for shift in range(near_heads):
            arrival(kind, 1, shift).wait_recv()
        spread(kind, 1 - mine)

    def halves(order):
        return mine if order == 0 else 1 - mine

    def is_end(at):
        return jnp.logical_or(at == 0, at == line - 1)

    def crosses(at, order):
        return True if order == 0 else jnp.logical_or(jnp.logical_not(is_end(at)), at == row)

    def relay(distance, order):
        half = halves(order)
        has_before, has_after = row >= distance, row + distance < line
        before, after = me - 2 * distance, me + 2 * distance

        @pl.when(has_before)
        def _():
            for kind in range(2):
                to_right(kind, before, half).wait_recv()

                @pl.when(has_right)
                def _():
                    to_right(kind, before, half).start()

                @pl.when(crosses(row - distance, order))
                def _():
                    to_side(kind, before, half).start()

        @pl.when(has_after)
        def _():
            for kind in range(2):
                to_left(kind, after, half).wait_recv()

                @pl.when(has_left)
                def _():
                    to_left(kind, after, half).start()

        if order == 0:

            @pl.when(jnp.logical_and(has_after, jnp.logical_not(has_before)))
            def _():
                for kind in range(2):
                    to_side(kind, after, half).start()
        else:

            @pl.when(jnp.logical_and(has_after, has_before))
            def _():
                for kind in range(2):
                    to_side(kind, after, mine).start()

            @pl.when(jnp.logical_and(has_after, crosses(row + distance, order)))
            def _():
                for kind in range(2):
                    to_side(kind, after, half).start()

    first_side, last_side = lax.rem(side, 2), 2 * (line - 1) + lax.rem(side, 2)

    def guests_start():
        for kind in range(2):

            @pl.when(row == 0)
            def _():
                to_right(kind, first_side, 1 - mine).start()

            @pl.when(row == line - 1)
            def _():
                to_left(kind, last_side, 1 - mine).start()

    def guests_pass(distance):
        for kind in range(2):

            @pl.when(row == distance)
            def _():
                to_right(kind, first_side, 1 - mine).wait_recv()

                @pl.when(has_right)
                def _():
                    to_right(kind, first_side, 1 - mine).start()

            @pl.when(row == line - 1 - distance)
            def _():
                to_left(kind, last_side, 1 - mine).wait_recv()

                @pl.when(has_left)
                def _():
                    to_left(kind, last_side, 1 - mine).start()

    ticks = qbuf.shape[0]

    def compute(chunks, first, before_tick):
        @pl.loop(0, ticks)
        def _(tick):
            before_tick(tick)
            start = index_ref[tick, me] * rows
            attend(tick, start, chunks, rows, first, qbuf, kbuf, vbuf, best_ref, accum_ref, None)

    def side_owner(place):
        return 2 * nearest(row, line, place) + lax.rem(side, 2)

    def own_owner(place):
        return 2 * nearest(row, line, place) + lax.rem(me, 2)

    def side_wait(owner):
        for order in range(2):

            @pl.when(crosses(lax.div(owner, 2), order))
            def _():
                for kind in range(2):
                    to_side(kind, owner, halves(order)).wait_recv()

    def first_events(tick):
        @pl.when(tick == 0)
        def _():
            relay(1, 0)

    relay_at = first_events
    pltpu.make_async_copy(slice_ref, index_ref, index_sem).wait()
    pltpu.make_async_copy(q_ref, qbuf, q_sem).wait()
    compute([me], True, relay_at)

    @pl.loop(1, line)
    def _(step):
        def events(tick):
            @pl.when(tick == 0)
            def _():
                relay(step, 1)
                side_wait(side_owner(step - 1))

                @pl.when(step == 1)
                def _():
                    guests_start()

                @pl.when(step > 1)
                def _():
                    guests_pass(step - 1)

            @pl.when(tick == 1)
            def _():
                relay(step + 1, 0)

        compute([own_owner(step), side_owner(step - 1)], False, events)

    side_wait(side_owner(line - 1))
    guests_pass(line - 1)

    for kind in range(2):
        for shift in range(1, near_heads):
            exchange(kind, 0, shift).wait_send()
        for shift in range(near_heads):
            exchange(kind, 1, shift).wait_send()

    @pl.loop(0, line)
    def _(index):
        owner = 2 * index + lax.rem(me, 2)
        for order in range(2):
            half = halves(order)
            for kind in range(2):

                @pl.when(crosses(index, order))
                def _():
                    to_side(kind, owner, half).wait_send()

                @pl.when(jnp.logical_and(has_right, index <= row))
                def _():
                    to_right(kind, owner, half).wait_send()

                @pl.when(jnp.logical_and(has_left, index >= row))
                def _():
                    to_left(kind, owner, half).wait_send()

    for kind in range(2):

        @pl.when(has_right)
        def _():
            to_right(kind, first_side, 1 - mine).wait_send()

        @pl.when(has_left)
        def _():
            to_left(kind, last_side, 1 - mine).wait_send()


def wide_join(parts, axis):
    return parts[0] if len(parts) == 1 else jnp.concatenate(parts, axis=axis)


def on_device(sizes, queries, keys, values, slice_index):
    n_pipe, n_head = sizes
    ticks, rows, columns = queries.shape
    shape = (rows * n_pipe, keys.shape[1] // n_head)
    slots = ticks * columns // HEAD_SIZE
    anywhere = pl.BlockSpec(memory_space=pltpu.HBM)
    dma = pltpu.SemaphoreType.DMA
    fast = pl.BlockSpec(memory_space=pltpu.VMEM)
    state = pl.pallas_call(
        lambda *refs: gather_kernel(n_pipe, n_head, *refs),
        out_shape=[
            pltpu.VMEM(shape, keys.dtype),
            pltpu.VMEM(shape, keys.dtype),
            pltpu.VMEM(queries.shape, queries.dtype),
            pltpu.VMEM((slots, rows, HEAD_SIZE), jnp.float32),
            pltpu.VMEM((slots, rows, 2 * HEAD_SIZE), jnp.float32),
        ],
        in_specs=[anywhere] * 4,
        out_specs=[fast] * 5,
        scratch_shapes=[
            pltpu.SMEM(slice_index.shape, slice_index.dtype),
            dma,
            dma((2,)),
            dma((2, 2, n_head // 2)),
            dma((2, 2, n_head // 2)),
            dma((2, n_pipe, 2)),
            dma((2, n_pipe, 2)),
            dma((2, n_pipe, 2)),
            dma((2, n_pipe, 2)),
            dma,
        ],
        compiler_params=pltpu.CompilerParams(collective_id=0, has_side_effects=True, vmem_limit_bytes=30 * 2 ** 20),
        name="gather",
    )(*(pltpu.with_memory_space_constraint(array, pltpu.HBM) for array in (slice_index, queries, keys, values)))
    return pl.pallas_call(
        lambda *refs: finish_kernel(n_pipe, *refs),
        out_shape=jax.ShapeDtypeStruct(queries.shape, queries.dtype),
        in_specs=[pl.BlockSpec(memory_space=pltpu.SMEM)] + [fast] * 5,
        out_specs=anywhere,
        scratch_shapes=[
            pltpu.VMEM(queries.shape, queries.dtype),
            dma((ticks, columns // HEAD_SIZE // STRIP)),
        ],
        compiler_params=pltpu.CompilerParams(vmem_limit_bytes=30 * 2 ** 20),
        name="finish",
    )(slice_index, *state)


def solution(mesh):
    sizes = (mesh.shape["pipe"], mesh.shape["head"])
    return jax.shard_map(
        lambda *arrays: on_device(sizes, *arrays),
        mesh=mesh,
        in_specs=(
            P(None, "pipe", "head"),
            P(("pipe", "head"), None),
            P(("pipe", "head"), None),
            P(),
        ),
        out_specs=P(None, "pipe", "head"),
        check_vma=False,
    )
```

```python
import math

import jax
import jax.numpy as jnp
from jax import lax
from jax.experimental import pallas as pl
from jax.experimental.pallas import tpu as pltpu
from jax.sharding import PartitionSpec as P

HEAD_SIZE = 128
NEG = -1e30
TO_EXP2 = HEAD_SIZE ** (-0.5) * math.log2(math.e)
MESH = pl.DeviceIdType.MESH
STRIP = 16


def scores_of(query, key_block):
    return lax.dot_general(query, key_block, (((1,), (1,)), ((), ())), preferred_element_type=jnp.float32)


def weigh(scores, peak, value_block):
    weights = jnp.exp2((scores - peak) * TO_EXP2).astype(jnp.bfloat16)
    ones = jnp.ones(value_block.shape, jnp.bfloat16)
    return jnp.dot(weights, jnp.concatenate([value_block, ones], axis=1), preferred_element_type=jnp.float32)


def wide(array, count):
    return jnp.concatenate([array] * count, axis=1)


def nearest(row, line, place):
    reach = jnp.minimum(row, line - 1 - row)
    offset = lax.div(place + 1, 2)
    near = jnp.where(lax.rem(place, 2) == 1, row - offset, row + offset)
    far = jnp.where(row < line - 1 - row, place, line - 1 - place)
    return jnp.where(place <= 2 * reach, near, far)


def attend(tick, start, firsts, rows, first, qbuf, kbuf, vbuf, best_ref, accum_ref, finish):
    half = rows // 2
    spans = [pl.ds(pl.multiple_of(at, half), half) for at in firsts]
    heads = qbuf.shape[2] // HEAD_SIZE
    group = heads // (kbuf.shape[1] // HEAD_SIZE)
    diff = lax.broadcasted_iota(jnp.int32, (rows, half), 1) - lax.broadcasted_iota(jnp.int32, (rows, half), 0)
    limits = wide_join([jnp.where(diff <= start - at, -NEG, NEG) for at in firsts], 1)

    def score(h):
        at = pl.ds(h * HEAD_SIZE, HEAD_SIZE)
        kv = pl.ds(h // group * HEAD_SIZE, HEAD_SIZE)
        block = wide_join([kbuf[span, kv] for span in spans], 0)
        return jnp.minimum(scores_of(qbuf[tick, :, at], block), limits)

    def rest(h, scores):
        kv = pl.ds(h // group * HEAD_SIZE, HEAD_SIZE)
        slot = tick * heads + h
        top = jnp.broadcast_to(jnp.max(scores, axis=-1, keepdims=True), (rows, HEAD_SIZE))
        if first:
            peak = top
        else:
            before = best_ref[slot]
            peak = jnp.maximum(before, top)
        block = wide_join([vbuf[span, kv] for span in spans], 0)
        result = weigh(scores, wide(peak, len(firsts) * half // HEAD_SIZE), block)
        if not first:
            result = result + accum_ref[slot] * wide(jnp.exp2((before - peak) * TO_EXP2), 2)
        if finish is not None:
            finish(h, result)
        else:
            best_ref[slot] = peak
            accum_ref[slot] = result

    scores = score(0)
    for h in range(heads):
        later = score(h + 1) if h + 1 < heads else None
        rest(h, scores)
        scores = later


def finish_kernel(n_pipe, n_head, index_ref, kbuf, vbuf, qbuf, best_ref, accum_ref, o_ref, obuf, out_sem):
    me = lax.axis_index("pipe")
    row, line = lax.div(me, 2), n_pipe // 2
    ticks, rows, q_width = qbuf.shape
    heads = q_width // HEAD_SIZE
    mine = lax.div(lax.axis_index("head"), n_head // 2)
    half = rows // 2
    own_base = (2 * nearest(row, line, line - 1) + lax.rem(me, 2)) * rows
    side_base = (2 * nearest(row, line, line - 2) + 1 - lax.rem(me, 2)) * rows
    last_base = (2 * nearest(row, line, line - 1) + 1 - lax.rem(me, 2)) * rows
    firsts = [own_base + (1 - mine) * half, side_base + (1 - mine) * half, last_base, last_base + half]
    least = jnp.minimum(jnp.minimum(firsts[0], firsts[1]), last_base)

    def strip_out(tick, strip):
        at = pl.ds(strip * STRIP * HEAD_SIZE, STRIP * HEAD_SIZE)
        return pltpu.make_async_copy(obuf.at[tick, :, at], o_ref.at[tick, :, at], out_sem.at[tick, strip])

    @pl.loop(0, ticks)
    def _(tick):
        def finish(h, result):
            obuf[tick, :, pl.ds(h * HEAD_SIZE, HEAD_SIZE)] = (result[:, :HEAD_SIZE] * pl.reciprocal(result[:, HEAD_SIZE:])).astype(obuf.dtype)
            if h % STRIP == STRIP - 1:
                strip_out(tick, h // STRIP).start()

        start = index_ref[tick, me] * rows

        @pl.when(least < start + rows)
        def _():
            attend(tick, start, firsts, rows, False, qbuf, kbuf, vbuf, best_ref, accum_ref, finish)

        @pl.when(least >= start + rows)
        def _():
            for h in range(heads):
                finish(h, accum_ref[tick * heads + h])

    for tick in range(ticks):
        for strip in range(heads // STRIP):
            strip_out(tick, strip).wait()


def gather_kernel(n_pipe, n_head, slice_ref, q_ref, k_ref, v_ref, kbuf, vbuf, qbuf, best_ref, accum_ref, index_ref,
                  index_sem, local_sem, head_send, head_recv, left_send, right_send, side_send, chunk_recv, q_sem):
    me = lax.axis_index("pipe")
    head = lax.axis_index("head")
    side = me + 1 - 2 * lax.rem(me, 2)
    row = lax.div(me, 2)
    line = n_pipe // 2
    has_left, has_right = row > 0, row < line - 1
    piece = k_ref.shape[0]
    rows = piece * n_head
    near_heads = n_head // 2
    half_rows = rows // 2
    mine = lax.div(head, near_heads)
    width = kbuf.shape[1]
    ins, bufs = (k_ref, v_ref), (kbuf, vbuf)

    barrier = pltpu.get_barrier_semaphore()
    for other in range(1, n_head):
        pl.semaphore_signal(barrier, inc=1, device_id=(me, lax.rem(head + other, n_head)), device_id_type=MESH)
    pl.semaphore_signal(barrier, inc=1, device_id=(side, head), device_id_type=MESH)

    @pl.when(has_left)
    def _():
        pl.semaphore_signal(barrier, inc=1, device_id=(me - 2, head), device_id_type=MESH)

    @pl.when(has_right)
    def _():
        pl.semaphore_signal(barrier, inc=1, device_id=(me + 2, head), device_id_type=MESH)

    def spot(kind, source):
        return bufs[kind].at[pl.ds(pl.multiple_of(me * rows + source * piece, piece), piece), :]

    def columns(kind, target):
        return ins[kind].at[:, pl.ds(pl.multiple_of(target * width, width), width)]

    def keep(kind):
        return pltpu.make_async_copy(columns(kind, head), spot(kind, head), local_sem.at[kind])

    for kind in range(2):
        keep(kind).start()
    pltpu.make_async_copy(slice_ref, index_ref, index_sem).start()
    pltpu.make_async_copy(q_ref, qbuf, q_sem).start()
    pl.semaphore_wait(barrier, n_head + jnp.where(has_left, 1, 0) + jnp.where(has_right, 1, 0))

    def chunk(kind, owner, half):
        return bufs[kind].at[pl.ds(pl.multiple_of(owner * rows + half * half_rows, half_rows), half_rows), :]

    def partner(far, shift):
        group = lax.rem(mine + far, 2)
        return group * near_heads + lax.rem(lax.rem(head, near_heads) + shift, near_heads)

    def exchange(kind, far, shift):
        target = partner(far, shift)
        return pltpu.make_async_remote_copy(
            columns(kind, target), spot(kind, head),
            head_send.at[kind, far, shift], head_recv.at[kind, far, shift],
            device_id=(me, target), device_id_type=MESH)

    def arrival(kind, far, shift):
        source = partner(far, near_heads - shift)
        return pltpu.make_async_remote_copy(
            columns(kind, head), spot(kind, source),
            head_send.at[kind, far, shift], head_recv.at[kind, far, shift],
            device_id=(me, source), device_id_type=MESH)

    def pass_on(kind, owner, half, target, sems):
        return pltpu.make_async_remote_copy(
            chunk(kind, owner, half), chunk(kind, owner, half), sems.at[kind, owner, half], chunk_recv.at[kind, owner, half],
            device_id=(target, head), device_id_type=MESH)

    def to_left(kind, owner, half):
        return pass_on(kind, owner, half, me - 2, left_send)

    def to_right(kind, owner, half):
        return pass_on(kind, owner, half, me + 2, right_send)

    def to_side(kind, owner, half):
        return pass_on(kind, owner, half, side, side_send)

    for kind in range(2):
        for shift in range(1, near_heads):
            exchange(kind, 0, shift).start()
    for kind in range(2):
        for shift in range(near_heads):
            exchange(kind, 1, shift).start()

    def spread(kind, half):
        to_side(kind, me, half).start()

        @pl.when(has_left)
        def _():
            to_left(kind, me, half).start()

        @pl.when(has_right)
        def _():
            to_right(kind, me, half).start()

    for kind in range(2):
        keep(kind).wait()
        for shift in range(1, near_heads):
            arrival(kind, 0, shift).wait_recv()
        spread(kind, mine)
    for kind in range(2):
        for shift in range(near_heads):
            arrival(kind, 1, shift).wait_recv()
        spread(kind, 1 - mine)

    def halves(order):
        return mine if order == 0 else 1 - mine

    def is_end(at):
        return jnp.logical_or(at == 0, at == line - 1)

    def crosses(at, order):
        return True if order == 0 else jnp.logical_or(jnp.logical_not(is_end(at)), at == row)

    def relay(distance, order):
        half = halves(order)
        has_before, has_after = row >= distance, row + distance < line
        before, after = me - 2 * distance, me + 2 * distance

        @pl.when(has_before)
        def _():
            for kind in range(2):
                to_right(kind, before, half).wait_recv()

                @pl.when(has_right)
                def _():
                    to_right(kind, before, half).start()

                @pl.when(crosses(row - distance, order))
                def _():
                    to_side(kind, before, half).start()

        @pl.when(has_after)
        def _():
            for kind in range(2):
                to_left(kind, after, half).wait_recv()

                @pl.when(has_left)
                def _():
                    to_left(kind, after, half).start()

        if order == 0:

            @pl.when(jnp.logical_and(has_after, jnp.logical_not(has_before)))
            def _():
                for kind in range(2):
                    to_side(kind, after, half).start()
        else:

            @pl.when(jnp.logical_and(has_after, has_before))
            def _():
                for kind in range(2):
                    to_side(kind, after, mine).start()

            @pl.when(jnp.logical_and(has_after, crosses(row + distance, order)))
            def _():
                for kind in range(2):
                    to_side(kind, after, half).start()

    first_side, last_side = lax.rem(side, 2), 2 * (line - 1) + lax.rem(side, 2)

    def guests_start():
        for kind in range(2):

            @pl.when(row == 0)
            def _():
                to_right(kind, first_side, 1 - mine).start()

            @pl.when(row == line - 1)
            def _():
                to_left(kind, last_side, 1 - mine).start()

    def guests(step):
        if isinstance(step, int):
            guests_start()
        else:
            guests_pass(step - 1)

    def guests_pass(distance):
        for kind in range(2):

            @pl.when(row == distance)
            def _():
                to_right(kind, first_side, 1 - mine).wait_recv()

                @pl.when(has_right)
                def _():
                    to_right(kind, first_side, 1 - mine).start()

            @pl.when(row == line - 1 - distance)
            def _():
                to_left(kind, last_side, 1 - mine).wait_recv()

                @pl.when(has_left)
                def _():
                    to_left(kind, last_side, 1 - mine).start()

    ticks = qbuf.shape[0]

    def compute(firsts, first, before_tick):
        @pl.loop(0, ticks)
        def _(tick):
            before_tick(tick)
            start = index_ref[tick, me] * rows
            attend(tick, start, firsts, rows, first, qbuf, kbuf, vbuf, best_ref, accum_ref, None)

    def side_owner(place):
        return 2 * nearest(row, line, place) + lax.rem(side, 2)

    def own_owner(place):
        return 2 * nearest(row, line, place) + lax.rem(me, 2)

    def side_wait(place, order):
        owner = side_owner(place)

        @pl.when(crosses(lax.div(owner, 2), order))
        def _():
            for kind in range(2):
                to_side(kind, owner, halves(order)).wait_recv()

    def part(owner, order):
        return owner * rows + halves(order) * half_rows

    def events(step):
        def before(tick):
            @pl.when(tick == 0)
            def _():
                relay(step, 0)
                side_wait(step - 1, 0)

            @pl.when(tick == 1)
            def _():
                relay(step, 1)
                side_wait(step - 1, 1)
                guests(step)

        return before

    pltpu.make_async_copy(slice_ref, index_ref, index_sem).wait()
    pltpu.make_async_copy(q_ref, qbuf, q_sem).wait()
    compute([part(me, 0), part(me, 1), part(own_owner(1), 0), part(side_owner(0), 0)], True, events(1))

    @pl.loop(2, line)
    def _(step):
        compute([
            part(own_owner(step - 1), 1), part(side_owner(step - 2), 1), part(own_owner(step), 0), part(side_owner(step - 1), 0)
        ], False, events(step))

    for order in range(2):
        side_wait(line - 1, order)
    guests_pass(line - 1)

    for kind in range(2):
        for shift in range(1, near_heads):
            exchange(kind, 0, shift).wait_send()
        for shift in range(near_heads):
            exchange(kind, 1, shift).wait_send()

    @pl.loop(0, line)
    def _(index):
        owner = 2 * index + lax.rem(me, 2)
        for order in range(2):
            half = halves(order)
            for kind in range(2):

                @pl.when(crosses(index, order))
                def _():
                    to_side(kind, owner, half).wait_send()

                @pl.when(jnp.logical_and(has_right, index <= row))
                def _():
                    to_right(kind, owner, half).wait_send()

                @pl.when(jnp.logical_and(has_left, index >= row))
                def _():
                    to_left(kind, owner, half).wait_send()

    for kind in range(2):

        @pl.when(has_right)
        def _():
            to_right(kind, first_side, 1 - mine).wait_send()

        @pl.when(has_left)
        def _():
            to_left(kind, last_side, 1 - mine).wait_send()


def wide_join(parts, axis):
    return parts[0] if len(parts) == 1 else jnp.concatenate(parts, axis=axis)


def on_device(sizes, queries, keys, values, slice_index):
    n_pipe, n_head = sizes
    ticks, rows, columns = queries.shape
    shape = (rows * n_pipe, keys.shape[1] // n_head)
    slots = ticks * columns // HEAD_SIZE
    anywhere = pl.BlockSpec(memory_space=pltpu.HBM)
    dma = pltpu.SemaphoreType.DMA
    fast = pl.BlockSpec(memory_space=pltpu.VMEM)
    state = pl.pallas_call(
        lambda *refs: gather_kernel(n_pipe, n_head, *refs),
        out_shape=[
            pltpu.VMEM(shape, keys.dtype),
            pltpu.VMEM(shape, keys.dtype),
            pltpu.VMEM(queries.shape, queries.dtype),
            pltpu.VMEM((slots, rows, HEAD_SIZE), jnp.float32),
            pltpu.VMEM((slots, rows, 2 * HEAD_SIZE), jnp.float32),
            pltpu.SMEM(slice_index.shape, slice_index.dtype),
        ],
        in_specs=[anywhere] * 4,
        out_specs=[fast] * 5 + [pl.BlockSpec(memory_space=pltpu.SMEM)],
        scratch_shapes=[
            dma,
            dma((2,)),
            dma((2, 2, n_head // 2)),
            dma((2, 2, n_head // 2)),
            dma((2, n_pipe, 2)),
            dma((2, n_pipe, 2)),
            dma((2, n_pipe, 2)),
            dma((2, n_pipe, 2)),
            dma,
        ],
        compiler_params=pltpu.CompilerParams(collective_id=0, has_side_effects=True, vmem_limit_bytes=30 * 2 ** 20),
        name="gather",
    )(*(pltpu.with_memory_space_constraint(array, pltpu.HBM) for array in (slice_index, queries, keys, values)))
    return pl.pallas_call(
        lambda *refs: finish_kernel(n_pipe, n_head, *refs),
        out_shape=jax.ShapeDtypeStruct(queries.shape, queries.dtype),
        in_specs=[pl.BlockSpec(memory_space=pltpu.SMEM)] + [fast] * 5,
        out_specs=anywhere,
        scratch_shapes=[
            pltpu.VMEM(queries.shape, queries.dtype),
            dma((ticks, columns // HEAD_SIZE // STRIP)),
        ],
        compiler_params=pltpu.CompilerParams(vmem_limit_bytes=30 * 2 ** 20),
        name="finish",
    )(state[5], *state[:5])


def solution(mesh):
    sizes = (mesh.shape["pipe"], mesh.shape["head"])
    return jax.shard_map(
        lambda *arrays: on_device(sizes, *arrays),
        mesh=mesh,
        in_specs=(
            P(None, "pipe", "head"),
            P(("pipe", "head"), None),
            P(("pipe", "head"), None),
            P(),
        ),
        out_specs=P(None, "pipe", "head"),
        check_vma=False,
    )
```

```python
import math

import jax
import jax.numpy as jnp
from jax import lax
from jax.experimental import pallas as pl
from jax.experimental.pallas import tpu as pltpu
from jax.sharding import PartitionSpec as P

HEAD_SIZE = 128
NEG = -1e30
TO_EXP2 = HEAD_SIZE ** (-0.5) * math.log2(math.e)
MESH = pl.DeviceIdType.MESH
STRIP = 4


def scores_of(query, key_block):
    return lax.dot_general(query, key_block, (((1,), (1,)), ((), ())), preferred_element_type=jnp.float32)


def weigh(scores, peak, value_block):
    weights = jnp.exp2((scores - peak) * TO_EXP2).astype(jnp.bfloat16)
    ones = jnp.ones(value_block.shape, jnp.bfloat16)
    return jnp.dot(weights, jnp.concatenate([value_block, ones], axis=1), preferred_element_type=jnp.float32)


def wide(array, count):
    return jnp.concatenate([array] * count, axis=1)


def nearest(row, line, place):
    reach = jnp.minimum(row, line - 1 - row)
    offset = lax.div(place + 1, 2)
    near = jnp.where(lax.rem(place, 2) == 1, row - offset, row + offset)
    far = jnp.where(row < line - 1 - row, place, line - 1 - place)
    return jnp.where(place <= 2 * reach, near, far)


def attend(tick, start, firsts, rows, qbuf, kbuf, vbuf, best_ref, accum_ref, finish):
    half = rows // 2
    spans = [pl.ds(pl.multiple_of(at, half), half) for at in firsts]
    heads = qbuf.shape[2] // HEAD_SIZE
    group = heads // (kbuf.shape[1] // HEAD_SIZE)
    diff = lax.broadcasted_iota(jnp.int32, (rows, half), 1) - lax.broadcasted_iota(jnp.int32, (rows, half), 0)
    limits = wide_join([jnp.where(diff <= start - at, -NEG, NEG) for at in firsts], 1)

    def score(h):
        at = pl.ds(h * HEAD_SIZE, HEAD_SIZE)
        kv = pl.ds(h // group * HEAD_SIZE, HEAD_SIZE)
        block = wide_join([kbuf[span, kv] for span in spans], 0)
        return jnp.minimum(scores_of(qbuf[tick, :, at], block), limits)

    def rest(h, scores):
        kv = pl.ds(h // group * HEAD_SIZE, HEAD_SIZE)
        slot = tick * heads + h
        top = jnp.broadcast_to(jnp.max(scores, axis=-1, keepdims=True), (rows, HEAD_SIZE))
        before = best_ref[slot]
        peak = jnp.maximum(before, top)
        block = wide_join([vbuf[span, kv] for span in spans], 0)
        result = weigh(scores, wide(peak, len(firsts) * half // HEAD_SIZE), block)
        result = result + accum_ref[slot] * wide(jnp.exp2((before - peak) * TO_EXP2), 2)
        if finish is not None:
            finish(h, result)
        else:
            best_ref[slot] = peak
            accum_ref[slot] = result

    scores = score(0)
    for h in range(heads):
        later = score(h + 1) if h + 1 < heads else None
        rest(h, scores)
        scores = later


def finish_kernel(n_pipe, n_head, index_ref, kbuf, vbuf, qbuf, best_ref, accum_ref, o_ref, obuf, out_sem):
    me = lax.axis_index("pipe")
    row, line = lax.div(me, 2), n_pipe // 2
    ticks, rows, q_width = qbuf.shape
    heads = q_width // HEAD_SIZE
    mine = lax.div(lax.axis_index("head"), n_head // 2)
    half = rows // 2
    own_base = (2 * nearest(row, line, line - 1) + lax.rem(me, 2)) * rows
    side_base = (2 * nearest(row, line, line - 2) + 1 - lax.rem(me, 2)) * rows
    last_base = (2 * nearest(row, line, line - 1) + 1 - lax.rem(me, 2)) * rows
    firsts = [own_base + (1 - mine) * half, side_base + (1 - mine) * half, last_base, last_base + half]
    least = jnp.minimum(jnp.minimum(firsts[0], firsts[1]), last_base)

    def strip_out(tick, strip):
        at = pl.ds(strip * STRIP * HEAD_SIZE, STRIP * HEAD_SIZE)
        return pltpu.make_async_copy(obuf.at[tick, :, at], o_ref.at[tick, :, at], out_sem.at[tick, strip])

    @pl.loop(0, ticks)
    def _(tick):
        def finish(h, result):
            obuf[tick, :, pl.ds(h * HEAD_SIZE, HEAD_SIZE)] = (result[:, :HEAD_SIZE] * pl.reciprocal(result[:, HEAD_SIZE:])).astype(obuf.dtype)
            if h % STRIP == STRIP - 1:
                strip_out(tick, h // STRIP).start()

        start = index_ref[tick, me] * rows

        @pl.when(least < start + rows)
        def _():
            attend(tick, start, firsts, rows, qbuf, kbuf, vbuf, best_ref, accum_ref, finish)

        @pl.when(least >= start + rows)
        def _():
            for h in range(heads):
                finish(h, accum_ref[tick * heads + h])

    for tick in range(ticks):
        for strip in range(heads // STRIP):
            strip_out(tick, strip).wait()


def gather_kernel(n_pipe, n_head, slice_ref, q_ref, k_ref, v_ref, kbuf, vbuf, qbuf, best_ref, accum_ref, index_ref,
                  index_sem, local_sem, head_send, head_recv, left_send, right_send, side_send, chunk_recv, q_sem):
    me = lax.axis_index("pipe")
    head = lax.axis_index("head")
    side = me + 1 - 2 * lax.rem(me, 2)
    row = lax.div(me, 2)
    line = n_pipe // 2
    has_left, has_right = row > 0, row < line - 1
    piece = k_ref.shape[0]
    rows = piece * n_head
    near_heads = n_head // 2
    half_rows = rows // 2
    mine = lax.div(head, near_heads)
    width = kbuf.shape[1]
    ins, bufs = (k_ref, v_ref), (kbuf, vbuf)

    barrier = pltpu.get_barrier_semaphore()
    for other in range(1, n_head):
        pl.semaphore_signal(barrier, inc=1, device_id=(me, lax.rem(head + other, n_head)), device_id_type=MESH)
    pl.semaphore_signal(barrier, inc=1, device_id=(side, head), device_id_type=MESH)

    @pl.when(has_left)
    def _():
        pl.semaphore_signal(barrier, inc=1, device_id=(me - 2, head), device_id_type=MESH)

    @pl.when(has_right)
    def _():
        pl.semaphore_signal(barrier, inc=1, device_id=(me + 2, head), device_id_type=MESH)

    def spot(kind, source):
        return bufs[kind].at[pl.ds(pl.multiple_of(me * rows + source * piece, piece), piece), :]

    def columns(kind, target):
        return ins[kind].at[:, pl.ds(pl.multiple_of(target * width, width), width)]

    def keep(kind):
        return pltpu.make_async_copy(columns(kind, head), spot(kind, head), local_sem.at[kind])

    for kind in range(2):
        keep(kind).start()
    pltpu.make_async_copy(slice_ref, index_ref, index_sem).start()
    pltpu.make_async_copy(q_ref, qbuf, q_sem).start()
    @pl.loop(0, best_ref.shape[0])
    def _(slot):
        best_ref[slot] = jnp.full(best_ref.shape[1:], NEG, best_ref.dtype)
        accum_ref[slot] = jnp.zeros(accum_ref.shape[1:], accum_ref.dtype)

    pl.semaphore_wait(barrier, n_head + jnp.where(has_left, 1, 0) + jnp.where(has_right, 1, 0))

    def chunk(kind, owner, half):
        return bufs[kind].at[pl.ds(pl.multiple_of(owner * rows + half * half_rows, half_rows), half_rows), :]

    def partner(far, shift):
        group = lax.rem(mine + far, 2)
        return group * near_heads + lax.rem(lax.rem(head, near_heads) + shift, near_heads)

    def exchange(kind, far, shift):
        target = partner(far, shift)
        return pltpu.make_async_remote_copy(
            columns(kind, target), spot(kind, head),
            head_send.at[kind, far, shift], head_recv.at[kind, far, shift],
            device_id=(me, target), device_id_type=MESH)

    def arrival(kind, far, shift):
        source = partner(far, near_heads - shift)
        return pltpu.make_async_remote_copy(
            columns(kind, head), spot(kind, source),
            head_send.at[kind, far, shift], head_recv.at[kind, far, shift],
            device_id=(me, source), device_id_type=MESH)

    def pass_on(kind, owner, half, target, sems):
        return pltpu.make_async_remote_copy(
            chunk(kind, owner, half), chunk(kind, owner, half), sems.at[kind, owner, half], chunk_recv.at[kind, owner, half],
            device_id=(target, head), device_id_type=MESH)

    def to_left(kind, owner, half):
        return pass_on(kind, owner, half, me - 2, left_send)

    def to_right(kind, owner, half):
        return pass_on(kind, owner, half, me + 2, right_send)

    def to_side(kind, owner, half):
        return pass_on(kind, owner, half, side, side_send)

    for kind in range(2):
        for shift in range(1, near_heads):
            exchange(kind, 0, shift).start()
    for kind in range(2):
        for shift in range(near_heads):
            exchange(kind, 1, shift).start()

    def spread(kind, half):
        to_side(kind, me, half).start()

        @pl.when(has_left)
        def _():
            to_left(kind, me, half).start()

        @pl.when(has_right)
        def _():
            to_right(kind, me, half).start()

    for kind in range(2):
        keep(kind).wait()
        for shift in range(1, near_heads):
            arrival(kind, 0, shift).wait_recv()
        spread(kind, mine)
    for kind in range(2):
        for shift in range(near_heads):
            arrival(kind, 1, shift).wait_recv()
        spread(kind, 1 - mine)

    def halves(order):
        return mine if order == 0 else 1 - mine

    def is_end(at):
        return jnp.logical_or(at == 0, at == line - 1)

    def crosses(at, order):
        return True if order == 0 else jnp.logical_or(jnp.logical_not(is_end(at)), at == row)

    def relay(distance, order):
        half = halves(order)
        has_before, has_after = row >= distance, row + distance < line
        before, after = me - 2 * distance, me + 2 * distance

        @pl.when(has_before)
        def _():
            for kind in range(2):
                to_right(kind, before, half).wait_recv()

                @pl.when(has_right)
                def _():
                    to_right(kind, before, half).start()

                @pl.when(crosses(row - distance, order))
                def _():
                    to_side(kind, before, half).start()

        @pl.when(has_after)
        def _():
            for kind in range(2):
                to_left(kind, after, half).wait_recv()

                @pl.when(has_left)
                def _():
                    to_left(kind, after, half).start()

        if order == 0:

            @pl.when(jnp.logical_and(has_after, jnp.logical_not(has_before)))
            def _():
                for kind in range(2):
                    to_side(kind, after, half).start()
        else:

            @pl.when(jnp.logical_and(has_after, has_before))
            def _():
                for kind in range(2):
                    to_side(kind, after, mine).start()

            @pl.when(jnp.logical_and(has_after, crosses(row + distance, order)))
            def _():
                for kind in range(2):
                    to_side(kind, after, half).start()

    first_side, last_side = lax.rem(side, 2), 2 * (line - 1) + lax.rem(side, 2)

    def guests_start():
        for kind in range(2):

            @pl.when(row == 0)
            def _():
                to_right(kind, first_side, 1 - mine).start()

            @pl.when(row == line - 1)
            def _():
                to_left(kind, last_side, 1 - mine).start()

    def guests(step):
        @pl.when(step == 1)
        def _():
            guests_start()

        @pl.when(step > 1)
        def _():
            guests_pass(step - 1)

    def guests_pass(distance):
        for kind in range(2):

            @pl.when(row == distance)
            def _():
                to_right(kind, first_side, 1 - mine).wait_recv()

                @pl.when(has_right)
                def _():
                    to_right(kind, first_side, 1 - mine).start()

            @pl.when(row == line - 1 - distance)
            def _():
                to_left(kind, last_side, 1 - mine).wait_recv()

                @pl.when(has_left)
                def _():
                    to_left(kind, last_side, 1 - mine).start()

    ticks = qbuf.shape[0]

    def compute(firsts, before_tick):
        @pl.loop(0, ticks)
        def _(tick):
            before_tick(tick)
            start = index_ref[tick, me] * rows
            attend(tick, start, firsts, rows, qbuf, kbuf, vbuf, best_ref, accum_ref, None)

    def side_owner(place):
        return 2 * nearest(row, line, place) + lax.rem(side, 2)

    def own_owner(place):
        return 2 * nearest(row, line, place) + lax.rem(me, 2)

    def side_wait(place, order):
        owner = side_owner(place)

        @pl.when(crosses(lax.div(owner, 2), order))
        def _():
            for kind in range(2):
                to_side(kind, owner, halves(order)).wait_recv()

    def part(owner, order):
        return owner * rows + halves(order) * half_rows

    def events(step):
        def before(tick):
            @pl.when(tick == 0)
            def _():
                relay(step, 0)
                side_wait(step - 1, 0)

            @pl.when(tick == 1)
            def _():
                relay(step, 1)
                side_wait(step - 1, 1)
                guests(step)

        return before

    pltpu.make_async_copy(slice_ref, index_ref, index_sem).wait()
    pltpu.make_async_copy(q_ref, qbuf, q_sem).wait()
    @pl.loop(1, line)
    def _(step):
        older = jnp.where(step == 1, part(me, 0), part(side_owner(step - 2), 1))
        compute([part(own_owner(step - 1), 1), older, part(own_owner(step), 0), part(side_owner(step - 1), 0)], events(step))

    for order in range(2):
        side_wait(line - 1, order)
    guests_pass(line - 1)

    for kind in range(2):
        for shift in range(1, near_heads):
            exchange(kind, 0, shift).wait_send()
        for shift in range(near_heads):
            exchange(kind, 1, shift).wait_send()

    @pl.loop(0, line)
    def _(index):
        owner = 2 * index + lax.rem(me, 2)
        for order in range(2):
            half = halves(order)
            for kind in range(2):

                @pl.when(crosses(index, order))
                def _():
                    to_side(kind, owner, half).wait_send()

                @pl.when(jnp.logical_and(has_right, index <= row))
                def _():
                    to_right(kind, owner, half).wait_send()

                @pl.when(jnp.logical_and(has_left, index >= row))
                def _():
                    to_left(kind, owner, half).wait_send()

    for kind in range(2):

        @pl.when(has_right)
        def _():
            to_right(kind, first_side, 1 - mine).wait_send()

        @pl.when(has_left)
        def _():
            to_left(kind, last_side, 1 - mine).wait_send()


def wide_join(parts, axis):
    return parts[0] if len(parts) == 1 else jnp.concatenate(parts, axis=axis)


def on_device(sizes, queries, keys, values, slice_index):
    n_pipe, n_head = sizes
    ticks, rows, columns = queries.shape
    shape = (rows * n_pipe, keys.shape[1] // n_head)
    slots = ticks * columns // HEAD_SIZE
    anywhere = pl.BlockSpec(memory_space=pltpu.HBM)
    dma = pltpu.SemaphoreType.DMA
    fast = pl.BlockSpec(memory_space=pltpu.VMEM)
    state = pl.pallas_call(
        lambda *refs: gather_kernel(n_pipe, n_head, *refs),
        out_shape=[
            pltpu.VMEM(shape, keys.dtype),
            pltpu.VMEM(shape, keys.dtype),
            pltpu.VMEM(queries.shape, queries.dtype),
            pltpu.VMEM((slots, rows, HEAD_SIZE), jnp.float32),
            pltpu.VMEM((slots, rows, 2 * HEAD_SIZE), jnp.float32),
            pltpu.SMEM(slice_index.shape, slice_index.dtype),
        ],
        in_specs=[anywhere] * 4,
        out_specs=[fast] * 5 + [pl.BlockSpec(memory_space=pltpu.SMEM)],
        scratch_shapes=[
            dma,
            dma((2,)),
            dma((2, 2, n_head // 2)),
            dma((2, 2, n_head // 2)),
            dma((2, n_pipe, 2)),
            dma((2, n_pipe, 2)),
            dma((2, n_pipe, 2)),
            dma((2, n_pipe, 2)),
            dma,
        ],
        compiler_params=pltpu.CompilerParams(collective_id=0, has_side_effects=True, vmem_limit_bytes=30 * 2 ** 20),
        name="gather",
    )(*(pltpu.with_memory_space_constraint(array, pltpu.HBM) for array in (slice_index, queries, keys, values)))
    return pl.pallas_call(
        lambda *refs: finish_kernel(n_pipe, n_head, *refs),
        out_shape=jax.ShapeDtypeStruct(queries.shape, queries.dtype),
        in_specs=[pl.BlockSpec(memory_space=pltpu.SMEM)] + [fast] * 5,
        out_specs=anywhere,
        scratch_shapes=[
            pltpu.VMEM(queries.shape, queries.dtype),
            dma((ticks, columns // HEAD_SIZE // STRIP)),
        ],
        compiler_params=pltpu.CompilerParams(vmem_limit_bytes=30 * 2 ** 20),
        name="finish",
    )(state[5], *state[:5])


def solution(mesh):
    sizes = (mesh.shape["pipe"], mesh.shape["head"])
    return jax.shard_map(
        lambda *arrays: on_device(sizes, *arrays),
        mesh=mesh,
        in_specs=(
            P(None, "pipe", "head"),
            P(("pipe", "head"), None),
            P(("pipe", "head"), None),
            P(),
        ),
        out_specs=P(None, "pipe", "head"),
        check_vma=False,
    )
```

```python
import math

import jax
import jax.numpy as jnp
from jax import lax
from jax.experimental import pallas as pl
from jax.experimental.pallas import tpu as pltpu
from jax.sharding import PartitionSpec as P

HEAD_SIZE = 128
NEG = -1e30
TO_EXP2 = HEAD_SIZE ** (-0.5) * math.log2(math.e)
MESH = pl.DeviceIdType.MESH
STRIP = 4


def scores_of(query, key_block):
    return lax.dot_general(query, key_block, (((1,), (1,)), ((), ())), preferred_element_type=jnp.float32)


def weigh(scores, peak, value_block):
    weights = jnp.exp2((scores - peak) * TO_EXP2).astype(jnp.bfloat16)
    ones = jnp.ones(value_block.shape, jnp.bfloat16)
    return jnp.dot(weights, jnp.concatenate([value_block, ones], axis=1), preferred_element_type=jnp.float32)


def wide(array, count):
    return jnp.concatenate([array] * count, axis=1)


def nearest(row, line, place):
    reach = jnp.minimum(row, line - 1 - row)
    offset = lax.div(place + 1, 2)
    near = jnp.where(lax.rem(place, 2) == 1, row - offset, row + offset)
    far = jnp.where(row < line - 1 - row, place, line - 1 - place)
    return jnp.where(place <= 2 * reach, near, far)


def attend(tick, start, firsts, rows, qbuf, kbuf, vbuf, best_ref, accum_ref, finish):
    half = rows // 2
    spans = [pl.ds(pl.multiple_of(at, half), half) for at in firsts]
    heads = qbuf.shape[2] // HEAD_SIZE
    group = heads // (kbuf.shape[1] // HEAD_SIZE)
    diff = lax.broadcasted_iota(jnp.int32, (rows, half), 1) - lax.broadcasted_iota(jnp.int32, (rows, half), 0)
    limits = wide_join([jnp.where(diff <= start - at, -NEG, NEG) for at in firsts], 1)

    def score(h):
        at = pl.ds(h * HEAD_SIZE, HEAD_SIZE)
        kv = pl.ds(h // group * HEAD_SIZE, HEAD_SIZE)
        block = wide_join([kbuf[span, kv] for span in spans], 0)
        return jnp.minimum(scores_of(qbuf[tick, :, at], block), limits)

    def rest(h, scores):
        kv = pl.ds(h // group * HEAD_SIZE, HEAD_SIZE)
        slot = tick * heads + h
        top = jnp.broadcast_to(jnp.max(scores, axis=-1, keepdims=True), (rows, HEAD_SIZE))
        before = best_ref[slot]
        peak = jnp.maximum(before, top)
        block = wide_join([vbuf[span, kv] for span in spans], 0)
        result = weigh(scores, wide(peak, len(firsts) * half // HEAD_SIZE), block)
        result = result + accum_ref[slot] * wide(jnp.exp2((before - peak) * TO_EXP2), 2)
        if finish is not None:
            finish(h, result)
        else:
            best_ref[slot] = peak
            accum_ref[slot] = result

    scores = score(0)
    for h in range(heads):
        later = score(h + 1) if h + 1 < heads else None
        rest(h, scores)
        scores = later


def finish_kernel(n_pipe, n_head, index_ref, kbuf, vbuf, qbuf, best_ref, accum_ref, o_ref, obuf, out_sem):
    me = lax.axis_index("pipe")
    row, line = lax.div(me, 2), n_pipe // 2
    ticks, rows, q_width = qbuf.shape
    heads = q_width // HEAD_SIZE
    mine = lax.div(lax.axis_index("head"), n_head // 2)
    half = rows // 2
    own_base = (2 * nearest(row, line, line - 1) + lax.rem(me, 2)) * rows
    side_base = (2 * nearest(row, line, line - 2) + 1 - lax.rem(me, 2)) * rows
    last_base = (2 * nearest(row, line, line - 1) + 1 - lax.rem(me, 2)) * rows
    firsts = [own_base + (1 - mine) * half, side_base + (1 - mine) * half, last_base, last_base + half]
    least = jnp.minimum(jnp.minimum(firsts[0], firsts[1]), last_base)

    def strip_out(tick, strip):
        at = pl.ds(strip * STRIP * HEAD_SIZE, STRIP * HEAD_SIZE)
        return pltpu.make_async_copy(obuf.at[tick, :, at], o_ref.at[tick, :, at], out_sem.at[tick, strip])

    @pl.loop(0, ticks)
    def _(tick):
        def finish(h, result):
            obuf[tick, :, pl.ds(h * HEAD_SIZE, HEAD_SIZE)] = (result[:, :HEAD_SIZE] * pl.reciprocal(result[:, HEAD_SIZE:])).astype(obuf.dtype)
            if h % STRIP == STRIP - 1:
                strip_out(tick, h // STRIP).start()

        start = index_ref[tick, me] * rows

        sees_last = last_base < start + rows

        @pl.when(sees_last)
        def _():
            attend(tick, start, firsts, rows, qbuf, kbuf, vbuf, best_ref, accum_ref, finish)

        @pl.when(jnp.logical_and(least < start + rows, jnp.logical_not(sees_last)))
        def _():
            attend(tick, start, firsts[:2], rows, qbuf, kbuf, vbuf, best_ref, accum_ref, finish)

        @pl.when(least >= start + rows)
        def _():
            for h in range(heads):
                finish(h, accum_ref[tick * heads + h])

    for tick in range(ticks):
        for strip in range(heads // STRIP):
            strip_out(tick, strip).wait()


def gather_kernel(n_pipe, n_head, slice_ref, q_ref, k_ref, v_ref, kbuf, vbuf, qbuf, best_ref, accum_ref, index_ref,
                  index_sem, kstage, vstage, stage_sem, local_sem, head_send, head_recv, left_send, right_send, side_send, chunk_recv, q_sem):
    me = lax.axis_index("pipe")
    head = lax.axis_index("head")
    side = me + 1 - 2 * lax.rem(me, 2)
    row = lax.div(me, 2)
    line = n_pipe // 2
    has_left, has_right = row > 0, row < line - 1
    piece = k_ref.shape[0]
    rows = piece * n_head
    near_heads = n_head // 2
    half_rows = rows // 2
    mine = lax.div(head, near_heads)
    width = kbuf.shape[1]
    inputs, ins, bufs = (k_ref, v_ref), (kstage, vstage), (kbuf, vbuf)

    barrier = pltpu.get_barrier_semaphore()
    for other in range(1, n_head):
        pl.semaphore_signal(barrier, inc=1, device_id=(me, lax.rem(head + other, n_head)), device_id_type=MESH)
    pl.semaphore_signal(barrier, inc=1, device_id=(side, head), device_id_type=MESH)

    @pl.when(has_left)
    def _():
        pl.semaphore_signal(barrier, inc=1, device_id=(me - 2, head), device_id_type=MESH)

    @pl.when(has_right)
    def _():
        pl.semaphore_signal(barrier, inc=1, device_id=(me + 2, head), device_id_type=MESH)

    def spot(kind, source):
        return bufs[kind].at[pl.ds(pl.multiple_of(me * rows + source * piece, piece), piece), :]

    def columns(kind, target):
        return ins[kind].at[:, pl.ds(pl.multiple_of(target * width, width), width)]

    def keep(kind):
        return pltpu.make_async_copy(columns(kind, head), spot(kind, head), local_sem.at[kind])

    for kind in range(2):
        pltpu.make_async_copy(inputs[kind], ins[kind], stage_sem.at[kind]).start()
    pltpu.make_async_copy(slice_ref, index_ref, index_sem).start()
    pltpu.make_async_copy(q_ref, qbuf, q_sem).start()
    @pl.loop(0, best_ref.shape[0])
    def _(slot):
        best_ref[slot] = jnp.full(best_ref.shape[1:], NEG, best_ref.dtype)
        accum_ref[slot] = jnp.zeros(accum_ref.shape[1:], accum_ref.dtype)

    for kind in range(2):
        pltpu.make_async_copy(inputs[kind], ins[kind], stage_sem.at[kind]).wait()
        keep(kind).start()
    pl.semaphore_wait(barrier, n_head + jnp.where(has_left, 1, 0) + jnp.where(has_right, 1, 0))

    def chunk(kind, owner, half):
        return bufs[kind].at[pl.ds(pl.multiple_of(owner * rows + half * half_rows, half_rows), half_rows), :]

    def partner(far, shift):
        group = lax.rem(mine + far, 2)
        return group * near_heads + lax.rem(lax.rem(head, near_heads) + shift, near_heads)

    def exchange(kind, far, shift):
        target = partner(far, shift)
        return pltpu.make_async_remote_copy(
            columns(kind, target), spot(kind, head),
            head_send.at[kind, far, shift], head_recv.at[kind, far, shift],
            device_id=(me, target), device_id_type=MESH)

    def arrival(kind, far, shift):
        source = partner(far, near_heads - shift)
        return pltpu.make_async_remote_copy(
            columns(kind, head), spot(kind, source),
            head_send.at[kind, far, shift], head_recv.at[kind, far, shift],
            device_id=(me, source), device_id_type=MESH)

    def pass_on(kind, owner, half, target, sems):
        return pltpu.make_async_remote_copy(
            chunk(kind, owner, half), chunk(kind, owner, half), sems.at[kind, owner, half], chunk_recv.at[kind, owner, half],
            device_id=(target, head), device_id_type=MESH)

    def to_left(kind, owner, half):
        return pass_on(kind, owner, half, me - 2, left_send)

    def to_right(kind, owner, half):
        return pass_on(kind, owner, half, me + 2, right_send)

    def to_side(kind, owner, half):
        return pass_on(kind, owner, half, side, side_send)

    for kind in range(2):
        for shift in range(1, near_heads):
            exchange(kind, 0, shift).start()
    for kind in range(2):
        for shift in range(near_heads):
            exchange(kind, 1, shift).start()

    def spread(kind, half):
        to_side(kind, me, half).start()

        @pl.when(has_left)
        def _():
            to_left(kind, me, half).start()

        @pl.when(has_right)
        def _():
            to_right(kind, me, half).start()

    for kind in range(2):
        keep(kind).wait()
        for shift in range(1, near_heads):
            arrival(kind, 0, shift).wait_recv()
        spread(kind, mine)
    for kind in range(2):
        for shift in range(near_heads):
            arrival(kind, 1, shift).wait_recv()
        spread(kind, 1 - mine)

    def halves(order):
        return mine if order == 0 else 1 - mine

    def is_end(at):
        return jnp.logical_or(at == 0, at == line - 1)

    def crosses(at, order):
        return True if order == 0 else jnp.logical_or(jnp.logical_not(is_end(at)), at == row)

    def relay(distance, order):
        half = halves(order)
        has_before, has_after = row >= distance, row + distance < line
        before, after = me - 2 * distance, me + 2 * distance

        @pl.when(has_before)
        def _():
            for kind in range(2):
                to_right(kind, before, half).wait_recv()

                @pl.when(has_right)
                def _():
                    to_right(kind, before, half).start()

                @pl.when(crosses(row - distance, order))
                def _():
                    to_side(kind, before, half).start()

        @pl.when(has_after)
        def _():
            for kind in range(2):
                to_left(kind, after, half).wait_recv()

                @pl.when(has_left)
                def _():
                    to_left(kind, after, half).start()

        if order == 0:

            @pl.when(jnp.logical_and(has_after, jnp.logical_not(has_before)))
            def _():
                for kind in range(2):
                    to_side(kind, after, half).start()
        else:

            @pl.when(jnp.logical_and(has_after, has_before))
            def _():
                for kind in range(2):
                    to_side(kind, after, mine).start()

            @pl.when(jnp.logical_and(has_after, crosses(row + distance, order)))
            def _():
                for kind in range(2):
                    to_side(kind, after, half).start()

    first_side, last_side = lax.rem(side, 2), 2 * (line - 1) + lax.rem(side, 2)

    def guests_start():
        for kind in range(2):

            @pl.when(row == 0)
            def _():
                to_right(kind, first_side, 1 - mine).start()

            @pl.when(row == line - 1)
            def _():
                to_left(kind, last_side, 1 - mine).start()

    def guests(step):
        @pl.when(step == 1)
        def _():
            guests_start()

        @pl.when(step > 1)
        def _():
            guests_pass(step - 1)

    def guests_pass(distance):
        for kind in range(2):

            @pl.when(row == distance)
            def _():
                to_right(kind, first_side, 1 - mine).wait_recv()

                @pl.when(has_right)
                def _():
                    to_right(kind, first_side, 1 - mine).start()

            @pl.when(row == line - 1 - distance)
            def _():
                to_left(kind, last_side, 1 - mine).wait_recv()

                @pl.when(has_left)
                def _():
                    to_left(kind, last_side, 1 - mine).start()

    ticks = qbuf.shape[0]

    def compute(firsts, before_tick):
        @pl.loop(0, ticks)
        def _(tick):
            before_tick(tick)
            start = index_ref[tick, me] * rows
            attend(tick, start, firsts, rows, qbuf, kbuf, vbuf, best_ref, accum_ref, None)

    def side_owner(place):
        return 2 * nearest(row, line, place) + lax.rem(side, 2)

    def own_owner(place):
        return 2 * nearest(row, line, place) + lax.rem(me, 2)

    def side_wait(place, order):
        owner = side_owner(place)

        @pl.when(crosses(lax.div(owner, 2), order))
        def _():
            for kind in range(2):
                to_side(kind, owner, halves(order)).wait_recv()

    def part(owner, order):
        return owner * rows + halves(order) * half_rows

    def events(step):
        def before(tick):
            @pl.when(tick == 0)
            def _():
                relay(step, 0)
                side_wait(step - 1, 0)

            @pl.when(tick == 1)
            def _():
                relay(step, 1)
                side_wait(step - 1, 1)
                guests(step)

        return before

    pltpu.make_async_copy(slice_ref, index_ref, index_sem).wait()
    pltpu.make_async_copy(q_ref, qbuf, q_sem).wait()
    @pl.loop(1, line)
    def _(step):
        older = jnp.where(step == 1, part(me, 0), part(side_owner(step - 2), 1))
        compute([part(own_owner(step - 1), 1), older, part(own_owner(step), 0), part(side_owner(step - 1), 0)], events(step))

    for order in range(2):
        side_wait(line - 1, order)
    guests_pass(line - 1)

    for kind in range(2):
        for shift in range(1, near_heads):
            exchange(kind, 0, shift).wait_send()
        for shift in range(near_heads):
            exchange(kind, 1, shift).wait_send()

    @pl.loop(0, line)
    def _(index):
        owner = 2 * index + lax.rem(me, 2)
        for order in range(2):
            half = halves(order)
            for kind in range(2):

                @pl.when(crosses(index, order))
                def _():
                    to_side(kind, owner, half).wait_send()

                @pl.when(jnp.logical_and(has_right, index <= row))
                def _():
                    to_right(kind, owner, half).wait_send()

                @pl.when(jnp.logical_and(has_left, index >= row))
                def _():
                    to_left(kind, owner, half).wait_send()

    for kind in range(2):

        @pl.when(has_right)
        def _():
            to_right(kind, first_side, 1 - mine).wait_send()

        @pl.when(has_left)
        def _():
            to_left(kind, last_side, 1 - mine).wait_send()


def wide_join(parts, axis):
    return parts[0] if len(parts) == 1 else jnp.concatenate(parts, axis=axis)


def on_device(sizes, queries, keys, values, slice_index):
    n_pipe, n_head = sizes
    ticks, rows, columns = queries.shape
    shape = (rows * n_pipe, keys.shape[1] // n_head)
    slots = ticks * columns // HEAD_SIZE
    anywhere = pl.BlockSpec(memory_space=pltpu.HBM)
    dma = pltpu.SemaphoreType.DMA
    fast = pl.BlockSpec(memory_space=pltpu.VMEM)
    state = pl.pallas_call(
        lambda *refs: gather_kernel(n_pipe, n_head, *refs),
        out_shape=[
            pltpu.VMEM(shape, keys.dtype),
            pltpu.VMEM(shape, keys.dtype),
            pltpu.VMEM(queries.shape, queries.dtype),
            pltpu.VMEM((slots, rows, HEAD_SIZE), jnp.float32),
            pltpu.VMEM((slots, rows, 2 * HEAD_SIZE), jnp.float32),
            pltpu.SMEM(slice_index.shape, slice_index.dtype),
        ],
        in_specs=[anywhere] * 4,
        out_specs=[fast] * 5 + [pl.BlockSpec(memory_space=pltpu.SMEM)],
        scratch_shapes=[
            dma,
            pltpu.VMEM(keys.shape, keys.dtype),
            pltpu.VMEM(values.shape, values.dtype),
            dma((2,)),
            dma((2,)),
            dma((2, 2, n_head // 2)),
            dma((2, 2, n_head // 2)),
            dma((2, n_pipe, 2)),
            dma((2, n_pipe, 2)),
            dma((2, n_pipe, 2)),
            dma((2, n_pipe, 2)),
            dma,
        ],
        compiler_params=pltpu.CompilerParams(collective_id=0, has_side_effects=True, vmem_limit_bytes=30 * 2 ** 20),
        name="gather",
    )(*(pltpu.with_memory_space_constraint(array, pltpu.HBM) for array in (slice_index, queries, keys, values)))
    return pl.pallas_call(
        lambda *refs: finish_kernel(n_pipe, n_head, *refs),
        out_shape=jax.ShapeDtypeStruct(queries.shape, queries.dtype),
        in_specs=[pl.BlockSpec(memory_space=pltpu.SMEM)] + [fast] * 5,
        out_specs=anywhere,
        scratch_shapes=[
            pltpu.VMEM(queries.shape, queries.dtype),
            dma((ticks, columns // HEAD_SIZE // STRIP)),
        ],
        compiler_params=pltpu.CompilerParams(vmem_limit_bytes=30 * 2 ** 20),
        name="finish",
    )(state[5], *state[:5])


def solution(mesh):
    sizes = (mesh.shape["pipe"], mesh.shape["head"])
    return jax.shard_map(
        lambda *arrays: on_device(sizes, *arrays),
        mesh=mesh,
        in_specs=(
            P(None, "pipe", "head"),
            P(("pipe", "head"), None),
            P(("pipe", "head"), None),
            P(),
        ),
        out_specs=P(None, "pipe", "head"),
        check_vma=False,
    )
```

```python
import functools
import math

import jax
import jax.numpy as jnp
from jax import lax
from jax.experimental import pallas as pl
from jax.experimental.pallas import tpu as pltpu
from jax.sharding import PartitionSpec as P

HEAD_SIZE = 128
NEG = -1e30
TO_EXP2 = HEAD_SIZE ** (-0.5) * math.log2(math.e)
MESH = pl.DeviceIdType.MESH
STRIP = 4


def scores_of(query, key_block):
    return lax.dot_general(query, key_block, (((1,), (1,)), ((), ())), preferred_element_type=jnp.float32)


def weigh(scores, peak, value_block):
    weights = jnp.exp2((scores - peak) * TO_EXP2).astype(jnp.bfloat16)
    ones = jnp.ones(value_block.shape, jnp.bfloat16)
    return jnp.dot(weights, jnp.concatenate([value_block, ones], axis=1), preferred_element_type=jnp.float32)


def wide(array, count):
    return jnp.concatenate([array] * count, axis=1)


def nearest(row, line, place):
    reach = jnp.minimum(row, line - 1 - row)
    offset = lax.div(place + 1, 2)
    near = jnp.where(lax.rem(place, 2) == 1, row - offset, row + offset)
    far = jnp.where(row < line - 1 - row, place, line - 1 - place)
    return jnp.where(place <= 2 * reach, near, far)


def plan(tick, start, firsts, rows, qbuf, kbuf, vbuf, best_ref, accum_ref, finish):
    half = rows // 2
    spans = [pl.ds(pl.multiple_of(at, half), half) for at in firsts]
    heads = qbuf.shape[2] // HEAD_SIZE
    group = heads // (kbuf.shape[1] // HEAD_SIZE)
    diff = lax.broadcasted_iota(jnp.int32, (rows, half), 1) - lax.broadcasted_iota(jnp.int32, (rows, half), 0)
    limits = wide_join([jnp.where(diff <= start - at, -NEG, NEG) for at in firsts], 1)

    def score(h):
        at = pl.ds(h * HEAD_SIZE, HEAD_SIZE)
        kv = pl.ds(h // group * HEAD_SIZE, HEAD_SIZE)
        block = wide_join([kbuf[span, kv] for span in spans], 0)
        return jnp.minimum(scores_of(qbuf[tick, :, at], block), limits)

    def rest(h, scores):
        kv = pl.ds(h // group * HEAD_SIZE, HEAD_SIZE)
        slot = tick * heads + h
        top = jnp.broadcast_to(jnp.max(scores, axis=-1, keepdims=True), (rows, HEAD_SIZE))
        before = best_ref[slot]
        peak = jnp.maximum(before, top)
        block = wide_join([vbuf[span, kv] for span in spans], 0)
        result = weigh(scores, wide(peak, len(firsts) * half // HEAD_SIZE), block)
        result = result + accum_ref[slot] * wide(jnp.exp2((before - peak) * TO_EXP2), 2)
        if finish is not None:
            finish(h, result)
        else:
            best_ref[slot] = peak
            accum_ref[slot] = result

    return [(functools.partial(score, h), functools.partial(rest, h)) for h in range(heads)]


def follow(steps):
    scores = steps[0][0]()
    for at, (_, rest) in enumerate(steps):
        later = steps[at + 1][0]() if at + 1 < len(steps) else None
        rest(scores)
        scores = later


def attend(*args):
    follow(plan(*args))


def finish_kernel(n_pipe, n_head, index_ref, kbuf, vbuf, qbuf, best_ref, accum_ref, o_ref, obuf, out_sem):
    me = lax.axis_index("pipe")
    row, line = lax.div(me, 2), n_pipe // 2
    ticks, rows, q_width = qbuf.shape
    heads = q_width // HEAD_SIZE
    mine = lax.div(lax.axis_index("head"), n_head // 2)
    half = rows // 2
    own_base = (2 * nearest(row, line, line - 1) + lax.rem(me, 2)) * rows
    side_base = (2 * nearest(row, line, line - 2) + 1 - lax.rem(me, 2)) * rows
    last_base = (2 * nearest(row, line, line - 1) + 1 - lax.rem(me, 2)) * rows
    firsts = [own_base + (1 - mine) * half, side_base + (1 - mine) * half, last_base, last_base + half]
    least = jnp.minimum(jnp.minimum(firsts[0], firsts[1]), last_base)

    def strip_out(tick, strip):
        at = pl.ds(strip * STRIP * HEAD_SIZE, STRIP * HEAD_SIZE)
        return pltpu.make_async_copy(obuf.at[tick, :, at], o_ref.at[tick, :, at], out_sem.at[tick, strip])

    def finish(tick, h, result):
        obuf[tick, :, pl.ds(h * HEAD_SIZE, HEAD_SIZE)] = (result[:, :HEAD_SIZE] * pl.reciprocal(result[:, HEAD_SIZE:])).astype(obuf.dtype)
        if h % STRIP == STRIP - 1:
            strip_out(tick, h // STRIP).start()

    def planned(tick, seen):
        return plan(tick, index_ref[tick, me] * rows, seen, rows, qbuf, kbuf, vbuf, best_ref, accum_ref, functools.partial(finish, tick))

    all_see = last_base < (index_ref[0, me] + 1) * rows
    for tick in range(1, ticks):
        all_see = jnp.logical_and(all_see, last_base < (index_ref[tick, me] + 1) * rows)

    @pl.when(all_see)
    def _():
        follow([step for tick in range(ticks) for step in planned(tick, firsts)])

    @pl.when(jnp.logical_not(all_see))
    def _():
        @pl.loop(0, ticks)
        def _(tick):
            start = index_ref[tick, me] * rows
            sees_last = last_base < start + rows

            @pl.when(sees_last)
            def _():
                follow(planned(tick, firsts))

            @pl.when(jnp.logical_and(least < start + rows, jnp.logical_not(sees_last)))
            def _():
                follow(planned(tick, firsts[:2]))

            @pl.when(least >= start + rows)
            def _():
                for h in range(heads):
                    finish(tick, h, accum_ref[tick * heads + h])

    for tick in range(ticks):
        for strip in range(heads // STRIP):
            strip_out(tick, strip).wait()


def gather_kernel(n_pipe, n_head, slice_ref, q_ref, k_ref, v_ref, kbuf, vbuf, qbuf, best_ref, accum_ref, index_ref,
                  index_sem, kstage, vstage, stage_sem, local_sem, head_send, head_recv, left_send, right_send, side_send, chunk_recv, q_sem):
    me = lax.axis_index("pipe")
    head = lax.axis_index("head")
    side = me + 1 - 2 * lax.rem(me, 2)
    row = lax.div(me, 2)
    line = n_pipe // 2
    has_left, has_right = row > 0, row < line - 1
    piece = k_ref.shape[0]
    rows = piece * n_head
    near_heads = n_head // 2
    half_rows = rows // 2
    mine = lax.div(head, near_heads)
    width = kbuf.shape[1]
    inputs, ins, bufs = (k_ref, v_ref), (kstage, vstage), (kbuf, vbuf)

    barrier = pltpu.get_barrier_semaphore()
    for other in range(1, n_head):
        pl.semaphore_signal(barrier, inc=1, device_id=(me, lax.rem(head + other, n_head)), device_id_type=MESH)
    pl.semaphore_signal(barrier, inc=1, device_id=(side, head), device_id_type=MESH)

    @pl.when(has_left)
    def _():
        pl.semaphore_signal(barrier, inc=1, device_id=(me - 2, head), device_id_type=MESH)

    @pl.when(has_right)
    def _():
        pl.semaphore_signal(barrier, inc=1, device_id=(me + 2, head), device_id_type=MESH)

    def spot(kind, source):
        return bufs[kind].at[pl.ds(pl.multiple_of(me * rows + source * piece, piece), piece), :]

    def columns(kind, target):
        return ins[kind].at[:, pl.ds(pl.multiple_of(target * width, width), width)]

    def keep(kind):
        return pltpu.make_async_copy(columns(kind, head), spot(kind, head), local_sem.at[kind])

    for kind in range(2):
        pltpu.make_async_copy(inputs[kind], ins[kind], stage_sem.at[kind]).start()
    pltpu.make_async_copy(slice_ref, index_ref, index_sem).start()
    pltpu.make_async_copy(q_ref, qbuf, q_sem).start()
    @pl.loop(0, best_ref.shape[0])
    def _(slot):
        best_ref[slot] = jnp.full(best_ref.shape[1:], NEG, best_ref.dtype)
        accum_ref[slot] = jnp.zeros(accum_ref.shape[1:], accum_ref.dtype)

    for kind in range(2):
        pltpu.make_async_copy(inputs[kind], ins[kind], stage_sem.at[kind]).wait()
        keep(kind).start()
    pl.semaphore_wait(barrier, n_head + jnp.where(has_left, 1, 0) + jnp.where(has_right, 1, 0))

    def chunk(kind, owner, half):
        return bufs[kind].at[pl.ds(pl.multiple_of(owner * rows + half * half_rows, half_rows), half_rows), :]

    def partner(far, shift):
        group = lax.rem(mine + far, 2)
        return group * near_heads + lax.rem(lax.rem(head, near_heads) + shift, near_heads)

    def exchange(kind, far, shift):
        target = partner(far, shift)
        return pltpu.make_async_remote_copy(
            columns(kind, target), spot(kind, head),
            head_send.at[kind, far, shift], head_recv.at[kind, far, shift],
            device_id=(me, target), device_id_type=MESH)

    def arrival(kind, far, shift):
        source = partner(far, near_heads - shift)
        return pltpu.make_async_remote_copy(
            columns(kind, head), spot(kind, source),
            head_send.at[kind, far, shift], head_recv.at[kind, far, shift],
            device_id=(me, source), device_id_type=MESH)

    def pass_on(kind, owner, half, target, sems):
        return pltpu.make_async_remote_copy(
            chunk(kind, owner, half), chunk(kind, owner, half), sems.at[kind, owner, half], chunk_recv.at[kind, owner, half],
            device_id=(target, head), device_id_type=MESH)

    def to_left(kind, owner, half):
        return pass_on(kind, owner, half, me - 2, left_send)

    def to_right(kind, owner, half):
        return pass_on(kind, owner, half, me + 2, right_send)

    def to_side(kind, owner, half):
        return pass_on(kind, owner, half, side, side_send)

    for kind in range(2):
        for shift in range(1, near_heads):
            exchange(kind, 0, shift).start()
    for kind in range(2):
        for shift in range(near_heads):
            exchange(kind, 1, shift).start()

    def spread(kind, half):
        to_side(kind, me, half).start()

        @pl.when(has_left)
        def _():
            to_left(kind, me, half).start()

        @pl.when(has_right)
        def _():
            to_right(kind, me, half).start()

    for kind in range(2):
        keep(kind).wait()
        for shift in range(1, near_heads):
            arrival(kind, 0, shift).wait_recv()
        spread(kind, mine)
    for kind in range(2):
        for shift in range(near_heads):
            arrival(kind, 1, shift).wait_recv()
        spread(kind, 1 - mine)

    def halves(order):
        return mine if order == 0 else 1 - mine

    def is_end(at):
        return jnp.logical_or(at == 0, at == line - 1)

    def crosses(at, order):
        return True if order == 0 else jnp.logical_or(jnp.logical_not(is_end(at)), at == row)

    def relay(distance, order):
        half = halves(order)
        has_before, has_after = row >= distance, row + distance < line
        before, after = me - 2 * distance, me + 2 * distance

        @pl.when(has_before)
        def _():
            for kind in range(2):
                to_right(kind, before, half).wait_recv()

                @pl.when(has_right)
                def _():
                    to_right(kind, before, half).start()

                @pl.when(crosses(row - distance, order))
                def _():
                    to_side(kind, before, half).start()

        @pl.when(has_after)
        def _():
            for kind in range(2):
                to_left(kind, after, half).wait_recv()

                @pl.when(has_left)
                def _():
                    to_left(kind, after, half).start()

        if order == 0:

            @pl.when(jnp.logical_and(has_after, jnp.logical_not(has_before)))
            def _():
                for kind in range(2):
                    to_side(kind, after, half).start()
        else:

            @pl.when(jnp.logical_and(has_after, has_before))
            def _():
                for kind in range(2):
                    to_side(kind, after, mine).start()

            @pl.when(jnp.logical_and(has_after, crosses(row + distance, order)))
            def _():
                for kind in range(2):
                    to_side(kind, after, half).start()

    first_side, last_side = lax.rem(side, 2), 2 * (line - 1) + lax.rem(side, 2)

    def guests_start():
        for kind in range(2):

            @pl.when(row == 0)
            def _():
                to_right(kind, first_side, 1 - mine).start()

            @pl.when(row == line - 1)
            def _():
                to_left(kind, last_side, 1 - mine).start()

    def guests(step):
        @pl.when(step == 1)
        def _():
            guests_start()

        @pl.when(step > 1)
        def _():
            guests_pass(step - 1)

    def guests_pass(distance):
        for kind in range(2):

            @pl.when(row == distance)
            def _():
                to_right(kind, first_side, 1 - mine).wait_recv()

                @pl.when(has_right)
                def _():
                    to_right(kind, first_side, 1 - mine).start()

            @pl.when(row == line - 1 - distance)
            def _():
                to_left(kind, last_side, 1 - mine).wait_recv()

                @pl.when(has_left)
                def _():
                    to_left(kind, last_side, 1 - mine).start()

    ticks = qbuf.shape[0]

    def compute(firsts, before_tick):
        @pl.loop(0, ticks)
        def _(tick):
            before_tick(tick)
            start = index_ref[tick, me] * rows
            attend(tick, start, firsts, rows, qbuf, kbuf, vbuf, best_ref, accum_ref, None)

    def side_owner(place):
        return 2 * nearest(row, line, place) + lax.rem(side, 2)

    def own_owner(place):
        return 2 * nearest(row, line, place) + lax.rem(me, 2)

    def side_wait(place, order):
        owner = side_owner(place)

        @pl.when(crosses(lax.div(owner, 2), order))
        def _():
            for kind in range(2):
                to_side(kind, owner, halves(order)).wait_recv()

    def part(owner, order):
        return owner * rows + halves(order) * half_rows

    def events(step):
        def before(tick):
            @pl.when(tick == 0)
            def _():
                relay(step, 0)
                side_wait(step - 1, 0)

            @pl.when(tick == 1)
            def _():
                relay(step, 1)
                side_wait(step - 1, 1)
                guests(step)

        return before

    pltpu.make_async_copy(slice_ref, index_ref, index_sem).wait()
    pltpu.make_async_copy(q_ref, qbuf, q_sem).wait()
    @pl.loop(1, line)
    def _(step):
        older = jnp.where(step == 1, part(me, 0), part(side_owner(step - 2), 1))
        compute([part(own_owner(step - 1), 1), older, part(own_owner(step), 0), part(side_owner(step - 1), 0)], events(step))

    for order in range(2):
        side_wait(line - 1, order)
    guests_pass(line - 1)

    for kind in range(2):
        for shift in range(1, near_heads):
            exchange(kind, 0, shift).wait_send()
        for shift in range(near_heads):
            exchange(kind, 1, shift).wait_send()

    @pl.loop(0, line)
    def _(index):
        owner = 2 * index + lax.rem(me, 2)
        for order in range(2):
            half = halves(order)
            for kind in range(2):

                @pl.when(crosses(index, order))
                def _():
                    to_side(kind, owner, half).wait_send()

                @pl.when(jnp.logical_and(has_right, index <= row))
                def _():
                    to_right(kind, owner, half).wait_send()

                @pl.when(jnp.logical_and(has_left, index >= row))
                def _():
                    to_left(kind, owner, half).wait_send()

    for kind in range(2):

        @pl.when(has_right)
        def _():
            to_right(kind, first_side, 1 - mine).wait_send()

        @pl.when(has_left)
        def _():
            to_left(kind, last_side, 1 - mine).wait_send()


def wide_join(parts, axis):
    return parts[0] if len(parts) == 1 else jnp.concatenate(parts, axis=axis)


def on_device(sizes, queries, keys, values, slice_index):
    n_pipe, n_head = sizes
    ticks, rows, columns = queries.shape
    shape = (rows * n_pipe, keys.shape[1] // n_head)
    slots = ticks * columns // HEAD_SIZE
    anywhere = pl.BlockSpec(memory_space=pltpu.HBM)
    dma = pltpu.SemaphoreType.DMA
    fast = pl.BlockSpec(memory_space=pltpu.VMEM)
    state = pl.pallas_call(
        lambda *refs: gather_kernel(n_pipe, n_head, *refs),
        out_shape=[
            pltpu.VMEM(shape, keys.dtype),
            pltpu.VMEM(shape, keys.dtype),
            pltpu.VMEM(queries.shape, queries.dtype),
            pltpu.VMEM((slots, rows, HEAD_SIZE), jnp.float32),
            pltpu.VMEM((slots, rows, 2 * HEAD_SIZE), jnp.float32),
            pltpu.SMEM(slice_index.shape, slice_index.dtype),
        ],
        in_specs=[anywhere] * 4,
        out_specs=[fast] * 5 + [pl.BlockSpec(memory_space=pltpu.SMEM)],
        scratch_shapes=[
            dma,
            pltpu.VMEM(keys.shape, keys.dtype),
            pltpu.VMEM(values.shape, values.dtype),
            dma((2,)),
            dma((2,)),
            dma((2, 2, n_head // 2)),
            dma((2, 2, n_head // 2)),
            dma((2, n_pipe, 2)),
            dma((2, n_pipe, 2)),
            dma((2, n_pipe, 2)),
            dma((2, n_pipe, 2)),
            dma,
        ],
        compiler_params=pltpu.CompilerParams(collective_id=0, has_side_effects=True, vmem_limit_bytes=30 * 2 ** 20),
        name="gather",
    )(*(pltpu.with_memory_space_constraint(array, pltpu.HBM) for array in (slice_index, queries, keys, values)))
    return pl.pallas_call(
        lambda *refs: finish_kernel(n_pipe, n_head, *refs),
        out_shape=jax.ShapeDtypeStruct(queries.shape, queries.dtype),
        in_specs=[pl.BlockSpec(memory_space=pltpu.SMEM)] + [fast] * 5,
        out_specs=anywhere,
        scratch_shapes=[
            pltpu.VMEM(queries.shape, queries.dtype),
            dma((ticks, columns // HEAD_SIZE // STRIP)),
        ],
        compiler_params=pltpu.CompilerParams(vmem_limit_bytes=30 * 2 ** 20),
        name="finish",
    )(state[5], *state[:5])


def solution(mesh):
    sizes = (mesh.shape["pipe"], mesh.shape["head"])
    return jax.shard_map(
        lambda *arrays: on_device(sizes, *arrays),
        mesh=mesh,
        in_specs=(
            P(None, "pipe", "head"),
            P(("pipe", "head"), None),
            P(("pipe", "head"), None),
            P(),
        ),
        out_specs=P(None, "pipe", "head"),
        check_vma=False,
    )
```

```python
import math

import jax
import jax.numpy as jnp
from jax import lax
from jax.experimental import pallas as pl
from jax.experimental.pallas import tpu as pltpu
from jax.sharding import PartitionSpec as P

HEAD_SIZE = 128
NEG = -1e30
TO_EXP2 = HEAD_SIZE ** (-0.5) * math.log2(math.e)
MESH = pl.DeviceIdType.MESH
STRIP = 4


def scores_of(query, key_block):
    return lax.dot_general(query, key_block, (((1,), (1,)), ((), ())), preferred_element_type=jnp.float32)


def weigh(scores, peak, value_block):
    weights = jnp.exp2((scores - peak) * TO_EXP2).astype(jnp.bfloat16)
    ones = jnp.ones(value_block.shape, jnp.bfloat16)
    return jnp.dot(weights, jnp.concatenate([value_block, ones], axis=1), preferred_element_type=jnp.float32)


def wide(array, count):
    return jnp.concatenate([array] * count, axis=1)


def nearest(row, line, place):
    reach = jnp.minimum(row, line - 1 - row)
    offset = lax.div(place + 1, 2)
    near = jnp.where(lax.rem(place, 2) == 1, row - offset, row + offset)
    far = jnp.where(row < line - 1 - row, place, line - 1 - place)
    return jnp.where(place <= 2 * reach, near, far)


def attend(tick, start, firsts, rows, qbuf, kbuf, vbuf, best_ref, accum_ref, finish):
    half = rows // 2
    spans = [pl.ds(pl.multiple_of(at, half), half) for at in firsts]
    heads = qbuf.shape[2] // HEAD_SIZE
    group = heads // (kbuf.shape[1] // HEAD_SIZE)
    diff = lax.broadcasted_iota(jnp.int32, (rows, half), 1) - lax.broadcasted_iota(jnp.int32, (rows, half), 0)
    limits = wide_join([jnp.where(diff <= start - at, -NEG, NEG) for at in firsts], 1)

    def score(h):
        at = pl.ds(h * HEAD_SIZE, HEAD_SIZE)
        kv = pl.ds(h // group * HEAD_SIZE, HEAD_SIZE)
        block = wide_join([kbuf[span, kv] for span in spans], 0)
        return jnp.minimum(scores_of(qbuf[tick, :, at], block), limits)

    def rest(h, scores):
        kv = pl.ds(h // group * HEAD_SIZE, HEAD_SIZE)
        slot = tick * heads + h
        top = jnp.broadcast_to(jnp.max(scores, axis=-1, keepdims=True), (rows, HEAD_SIZE))
        before = best_ref[slot]
        peak = jnp.maximum(before, top)
        block = wide_join([vbuf[span, kv] for span in spans], 0)
        result = weigh(scores, wide(peak, len(firsts) * half // HEAD_SIZE), block)
        result = result + accum_ref[slot] * wide(jnp.exp2((before - peak) * TO_EXP2), 2)
        if finish is not None:
            finish(h, result)
        else:
            best_ref[slot] = peak
            accum_ref[slot] = result

    scores = score(0)
    for h in range(heads):
        later = score(h + 1) if h + 1 < heads else None
        rest(h, scores)
        scores = later


def finish_kernel(n_pipe, n_head, index_ref, kbuf, vbuf, qbuf, best_ref, accum_ref, o_ref, obuf, out_sem):
    me = lax.axis_index("pipe")
    row, line = lax.div(me, 2), n_pipe // 2
    ticks, rows, q_width = qbuf.shape
    heads = q_width // HEAD_SIZE
    mine = lax.div(lax.axis_index("head"), n_head // 2)
    half = rows // 2
    own_base = (2 * nearest(row, line, line - 1) + lax.rem(me, 2)) * rows
    side_base = (2 * nearest(row, line, line - 2) + 1 - lax.rem(me, 2)) * rows
    last_base = (2 * nearest(row, line, line - 1) + 1 - lax.rem(me, 2)) * rows
    firsts = [own_base + (1 - mine) * half, side_base + (1 - mine) * half, last_base, last_base + half]
    least = jnp.minimum(jnp.minimum(firsts[0], firsts[1]), last_base)

    def strip_out(tick, strip):
        at = pl.ds(strip * STRIP * HEAD_SIZE, STRIP * HEAD_SIZE)
        return pltpu.make_async_copy(obuf.at[tick, :, at], o_ref.at[tick, :, at], out_sem.at[tick, strip])

    @pl.loop(0, ticks)
    def _(tick):
        def finish(h, result):
            obuf[tick, :, pl.ds(h * HEAD_SIZE, HEAD_SIZE)] = (result[:, :HEAD_SIZE] * pl.reciprocal(result[:, HEAD_SIZE:])).astype(obuf.dtype)
            if h % STRIP == STRIP - 1:
                strip_out(tick, h // STRIP).start()

        start = index_ref[tick, me] * rows

        sees_last = last_base < start + rows

        @pl.when(sees_last)
        def _():
            attend(tick, start, firsts, rows, qbuf, kbuf, vbuf, best_ref, accum_ref, finish)

        @pl.when(jnp.logical_and(least < start + rows, jnp.logical_not(sees_last)))
        def _():
            attend(tick, start, firsts[:2], rows, qbuf, kbuf, vbuf, best_ref, accum_ref, finish)

        @pl.when(least >= start + rows)
        def _():
            for h in range(heads):
                finish(h, accum_ref[tick * heads + h])

    for tick in range(ticks):
        for strip in range(heads // STRIP):
            strip_out(tick, strip).wait()


def gather_kernel(n_pipe, n_head, slice_ref, q_ref, k_ref, v_ref, kbuf, vbuf, qbuf, best_ref, accum_ref, index_ref,
                  index_sem, kstage, vstage, stage_sem, local_sem, head_send, head_recv, left_send, right_send, side_send, chunk_recv, q_sem):
    me = lax.axis_index("pipe")
    head = lax.axis_index("head")
    side = me + 1 - 2 * lax.rem(me, 2)
    row = lax.div(me, 2)
    line = n_pipe // 2
    has_left, has_right = row > 0, row < line - 1
    piece = k_ref.shape[0]
    rows = piece * n_head
    near_heads = n_head // 2
    half_rows = rows // 2
    mine = lax.div(head, near_heads)
    width = kbuf.shape[1]
    inputs, ins, bufs = (k_ref, v_ref), (kstage, vstage), (kbuf, vbuf)

    barrier = pltpu.get_barrier_semaphore()
    for other in range(1, n_head):
        pl.semaphore_signal(barrier, inc=1, device_id=(me, lax.rem(head + other, n_head)), device_id_type=MESH)
    pl.semaphore_signal(barrier, inc=1, device_id=(side, head), device_id_type=MESH)

    @pl.when(has_left)
    def _():
        pl.semaphore_signal(barrier, inc=1, device_id=(me - 2, head), device_id_type=MESH)

    @pl.when(has_right)
    def _():
        pl.semaphore_signal(barrier, inc=1, device_id=(me + 2, head), device_id_type=MESH)

    def spot(kind, source):
        return bufs[kind].at[pl.ds(pl.multiple_of(me * rows + source * piece, piece), piece), :]

    def columns(kind, target):
        return ins[kind].at[:, pl.ds(pl.multiple_of(target * width, width), width)]

    def keep(kind):
        return pltpu.make_async_copy(columns(kind, head), spot(kind, head), local_sem.at[kind])

    for kind in range(2):
        pltpu.make_async_copy(inputs[kind], ins[kind], stage_sem.at[kind]).start()
    pltpu.make_async_copy(slice_ref, index_ref, index_sem).start()
    pltpu.make_async_copy(q_ref, qbuf, q_sem).start()
    @pl.loop(0, best_ref.shape[0])
    def _(slot):
        best_ref[slot] = jnp.full(best_ref.shape[1:], NEG, best_ref.dtype)
        accum_ref[slot] = jnp.zeros(accum_ref.shape[1:], accum_ref.dtype)

    for kind in range(2):
        pltpu.make_async_copy(inputs[kind], ins[kind], stage_sem.at[kind]).wait()
        keep(kind).start()
    pl.semaphore_wait(barrier, n_head + jnp.where(has_left, 1, 0) + jnp.where(has_right, 1, 0))

    def chunk(kind, owner, half):
        return bufs[kind].at[pl.ds(pl.multiple_of(owner * rows + half * half_rows, half_rows), half_rows), :]

    def partner(far, shift):
        group = lax.rem(mine + far, 2)
        return group * near_heads + lax.rem(lax.rem(head, near_heads) + shift, near_heads)

    def exchange(kind, far, shift):
        target = partner(far, shift)
        return pltpu.make_async_remote_copy(
            columns(kind, target), spot(kind, head),
            head_send.at[kind, far, shift], head_recv.at[kind, far, shift],
            device_id=(me, target), device_id_type=MESH)

    def arrival(kind, far, shift):
        source = partner(far, near_heads - shift)
        return pltpu.make_async_remote_copy(
            columns(kind, head), spot(kind, source),
            head_send.at[kind, far, shift], head_recv.at[kind, far, shift],
            device_id=(me, source), device_id_type=MESH)

    def pass_on(kind, owner, half, target, sems):
        return pltpu.make_async_remote_copy(
            chunk(kind, owner, half), chunk(kind, owner, half), sems.at[kind, owner, half], chunk_recv.at[kind, owner, half],
            device_id=(target, head), device_id_type=MESH)

    def to_left(kind, owner, half):
        return pass_on(kind, owner, half, me - 2, left_send)

    def to_right(kind, owner, half):
        return pass_on(kind, owner, half, me + 2, right_send)

    def to_side(kind, owner, half):
        return pass_on(kind, owner, half, side, side_send)

    for kind in range(2):
        for shift in range(1, near_heads):
            exchange(kind, 0, shift).start()
    for kind in range(2):
        for shift in range(near_heads):
            exchange(kind, 1, shift).start()

    def spread(kind, half):
        to_side(kind, me, half).start()

        @pl.when(has_left)
        def _():
            to_left(kind, me, half).start()

        @pl.when(has_right)
        def _():
            to_right(kind, me, half).start()

    for kind in range(2):
        keep(kind).wait()
        for shift in range(1, near_heads):
            arrival(kind, 0, shift).wait_recv()
        spread(kind, mine)
    for kind in range(2):
        for shift in range(near_heads):
            arrival(kind, 1, shift).wait_recv()
        spread(kind, 1 - mine)

    def halves(order):
        return mine if order == 0 else 1 - mine

    def is_end(at):
        return jnp.logical_or(at == 0, at == line - 1)

    def crosses(at, order):
        return True if order == 0 else jnp.logical_or(jnp.logical_not(is_end(at)), at == row)

    def relay(distance, order):
        half = halves(order)
        has_before, has_after = row >= distance, row + distance < line
        before, after = me - 2 * distance, me + 2 * distance

        @pl.when(has_before)
        def _():
            for kind in range(2):
                to_right(kind, before, half).wait_recv()

                @pl.when(has_right)
                def _():
                    to_right(kind, before, half).start()

                @pl.when(crosses(row - distance, order))
                def _():
                    to_side(kind, before, half).start()

        @pl.when(has_after)
        def _():
            for kind in range(2):
                to_left(kind, after, half).wait_recv()

                @pl.when(has_left)
                def _():
                    to_left(kind, after, half).start()

        if order == 0:

            @pl.when(jnp.logical_and(has_after, jnp.logical_not(has_before)))
            def _():
                for kind in range(2):
                    to_side(kind, after, half).start()
        else:

            @pl.when(jnp.logical_and(has_after, has_before))
            def _():
                for kind in range(2):
                    to_side(kind, after, mine).start()

            @pl.when(jnp.logical_and(has_after, crosses(row + distance, order)))
            def _():
                for kind in range(2):
                    to_side(kind, after, half).start()

    first_side, last_side = lax.rem(side, 2), 2 * (line - 1) + lax.rem(side, 2)

    def guests_start():
        for kind in range(2):

            @pl.when(row == 0)
            def _():
                to_right(kind, first_side, 1 - mine).start()

            @pl.when(row == line - 1)
            def _():
                to_left(kind, last_side, 1 - mine).start()

    def guests(step):
        @pl.when(step == 1)
        def _():
            guests_start()

        @pl.when(step > 1)
        def _():
            guests_pass(step - 1)

    def guests_pass(distance):
        for kind in range(2):

            @pl.when(row == distance)
            def _():
                to_right(kind, first_side, 1 - mine).wait_recv()

                @pl.when(has_right)
                def _():
                    to_right(kind, first_side, 1 - mine).start()

            @pl.when(row == line - 1 - distance)
            def _():
                to_left(kind, last_side, 1 - mine).wait_recv()

                @pl.when(has_left)
                def _():
                    to_left(kind, last_side, 1 - mine).start()

    ticks = qbuf.shape[0]

    def compute(firsts, before_tick):
        @pl.loop(0, ticks)
        def _(tick):
            before_tick(tick)
            start = index_ref[tick, me] * rows
            attend(tick, start, firsts, rows, qbuf, kbuf, vbuf, best_ref, accum_ref, None)

    def side_owner(place):
        return 2 * nearest(row, line, place) + lax.rem(side, 2)

    def own_owner(place):
        return 2 * nearest(row, line, place) + lax.rem(me, 2)

    def side_wait(place, order):
        owner = side_owner(place)

        @pl.when(crosses(lax.div(owner, 2), order))
        def _():
            for kind in range(2):
                to_side(kind, owner, halves(order)).wait_recv()

    def part(owner, order):
        return owner * rows + halves(order) * half_rows

    def events(step):
        def before(tick):
            @pl.when(tick == 0)
            def _():
                relay(step, 0)
                side_wait(step - 1, 0)

            @pl.when(tick == 1)
            def _():
                relay(step, 1)
                side_wait(step - 1, 1)
                guests(step)

        return before

    pltpu.make_async_copy(slice_ref, index_ref, index_sem).wait()
    pltpu.make_async_copy(q_ref, qbuf, q_sem).wait()
    @pl.loop(1, line)
    def _(step):
        older = jnp.where(step == 1, part(me, 0), part(side_owner(step - 2), 1))
        compute([part(own_owner(step - 1), 1), older, part(own_owner(step), 0), part(side_owner(step - 1), 0)], events(step))

    for kind in range(2):
        for shift in range(1, near_heads):
            exchange(kind, 0, shift).wait_send()
        for shift in range(near_heads):
            exchange(kind, 1, shift).wait_send()

    @pl.loop(0, line)
    def _(index):
        owner = 2 * index + lax.rem(me, 2)
        for order in range(2):
            half = halves(order)
            for kind in range(2):

                @pl.when(crosses(index, order))
                def _():
                    to_side(kind, owner, half).wait_send()

                @pl.when(jnp.logical_and(has_right, index <= row))
                def _():
                    to_right(kind, owner, half).wait_send()

                @pl.when(jnp.logical_and(has_left, index >= row))
                def _():
                    to_left(kind, owner, half).wait_send()

    for kind in range(2):

        @pl.when(has_right)
        def _():
            to_right(kind, first_side, 1 - mine).wait_send()

        @pl.when(has_left)
        def _():
            to_left(kind, last_side, 1 - mine).wait_send()

    for order in range(2):
        side_wait(line - 1, order)
    guests_pass(line - 1)


def wide_join(parts, axis):
    return parts[0] if len(parts) == 1 else jnp.concatenate(parts, axis=axis)


def on_device(sizes, queries, keys, values, slice_index):
    n_pipe, n_head = sizes
    ticks, rows, columns = queries.shape
    shape = (rows * n_pipe, keys.shape[1] // n_head)
    slots = ticks * columns // HEAD_SIZE
    anywhere = pl.BlockSpec(memory_space=pltpu.HBM)
    dma = pltpu.SemaphoreType.DMA
    fast = pl.BlockSpec(memory_space=pltpu.VMEM)
    state = pl.pallas_call(
        lambda *refs: gather_kernel(n_pipe, n_head, *refs),
        out_shape=[
            pltpu.VMEM(shape, keys.dtype),
            pltpu.VMEM(shape, keys.dtype),
            pltpu.VMEM(queries.shape, queries.dtype),
            pltpu.VMEM((slots, rows, HEAD_SIZE), jnp.float32),
            pltpu.VMEM((slots, rows, 2 * HEAD_SIZE), jnp.float32),
            pltpu.SMEM(slice_index.shape, slice_index.dtype),
        ],
        in_specs=[anywhere] * 4,
        out_specs=[fast] * 5 + [pl.BlockSpec(memory_space=pltpu.SMEM)],
        scratch_shapes=[
            dma,
            pltpu.VMEM(keys.shape, keys.dtype),
            pltpu.VMEM(values.shape, values.dtype),
            dma((2,)),
            dma((2,)),
            dma((2, 2, n_head // 2)),
            dma((2, 2, n_head // 2)),
            dma((2, n_pipe, 2)),
            dma((2, n_pipe, 2)),
            dma((2, n_pipe, 2)),
            dma((2, n_pipe, 2)),
            dma,
        ],
        compiler_params=pltpu.CompilerParams(collective_id=0, has_side_effects=True, vmem_limit_bytes=30 * 2 ** 20),
        name="gather",
    )(*(pltpu.with_memory_space_constraint(array, pltpu.HBM) for array in (slice_index, queries, keys, values)))
    return pl.pallas_call(
        lambda *refs: finish_kernel(n_pipe, n_head, *refs),
        out_shape=jax.ShapeDtypeStruct(queries.shape, queries.dtype),
        in_specs=[pl.BlockSpec(memory_space=pltpu.SMEM)] + [fast] * 5,
        out_specs=anywhere,
        scratch_shapes=[
            pltpu.VMEM(queries.shape, queries.dtype),
            dma((ticks, columns // HEAD_SIZE // STRIP)),
        ],
        compiler_params=pltpu.CompilerParams(vmem_limit_bytes=30 * 2 ** 20),
        name="finish",
    )(state[5], *state[:5])


def solution(mesh):
    sizes = (mesh.shape["pipe"], mesh.shape["head"])
    return jax.shard_map(
        lambda *arrays: on_device(sizes, *arrays),
        mesh=mesh,
        in_specs=(
            P(None, "pipe", "head"),
            P(("pipe", "head"), None),
            P(("pipe", "head"), None),
            P(),
        ),
        out_specs=P(None, "pipe", "head"),
        check_vma=False,
    )
```
